256 devices in a mesh: grp: 4 (over y), lev: 64 (over x, z, core).
Axes of the slice: x: 4, y: 4, z: 8, core: 2. Of those that a mesh axis runs over, the one named last changes fastest.
Arguments:
- up_tiles: bfloat16 [512, 24, 128, 128], P(('grp', 'lev')), may hold values from -0.3125 to 0.3125
- up_at: int32 [512, 24], P(('grp', 'lev')), may hold values from 0 to 63, as said below
- down_tiles: bfloat16 [512, 24, 128, 128], P(('grp', 'lev')), may hold values from -0.3125 to 0.3125
- down_at: int32 [512, 24], P(('grp', 'lev')), may hold values from 0 to 63, as said below
- diag_tiles: bfloat16 [256, 24, 128, 128], P(('grp', 'lev')), may hold values from -6 to 6
- diag_at: int32 [256, 24], P(('grp', 'lev')), may hold values from 0 to 63, as said below
- odd_inverse: bfloat16 [256, 1024, 1024], P(('grp', 'lev')), may hold values from -6 to 6
Outputs:
- new_diag: bfloat16 [256, 1024, 1024], P(('grp', 'lev'))
- new_up: bfloat16 [256, 1024, 1024], P(('grp', 'lev'))
- new_down: bfloat16 [256, 1024, 1024], P(('grp', 'lev'))
- partial_sums: float32 [256, 1024], P(('grp', 'lev'))
The draws below stay inside these ranges and needn't reach their ends.
Inputs may be any that keep to these rules, and one draw needn't show every extreme that they name: `up_at`: within one row the 24 tile positions are distinct. `down_at`: within one row the 24 tile positions are distinct. `diag_at`: within one row the 24 tile positions are distinct.
All inputs are finite; a program needn't handle non-finite values.
Results may differ from the reference program's by a relative error of at most 0.007.
Values may be sent and summed in bfloat16 or wider, within the bound.
A program may use at most 128 MiB of HBM per device.

```python
import jax
import jax.numpy as jnp
from jax import lax

TILE = 128
NT = 8
P_SIZE = 1024
KT = 24
PAIRS = 256
LEVELS = 512


def tile_positions(base_key, row_count):
    subkeys = jax.random.split(base_key, row_count)

    def one_row(subkey):
        return jax.random.permutation(subkey, NT * NT)[:KT]
    return jax.vmap(one_row)(subkeys).astype(jnp.int32)


def draw_up_at(key, part):
    return tile_positions(jax.random.fold_in(key, 11), LEVELS)


def draw_down_at(key, part):
    return tile_positions(jax.random.fold_in(key, 12), LEVELS)


def draw_diag_at(key, part):
    return tile_positions(jax.random.fold_in(key, 13), PAIRS)


def block_scale(stream_key, shape, cuts, smallest, largest):
    level = 1.0
    for axis_at, blocks in cuts:
        draws = jax.random.uniform(jax.random.fold_in(jax.random.fold_in(stream_key, 6), axis_at), (blocks,), jnp.float32, smallest / len(cuts), largest / len(cuts))
        level = level * jnp.repeat(jnp.exp(draws), shape[axis_at] // blocks).reshape((-1,) + (1,) * (len(shape) - 1 - axis_at))
    return level


def gaussian(rng, shape, scale, most, cuts=(), kind=jnp.bfloat16):
    level = block_scale(rng, shape, cuts, -0.22, 0.18) if cuts else 1.0
    values = jax.random.normal(rng, shape, jnp.float32) * scale * level
    return jnp.minimum(jnp.maximum(values, -most), most).astype(kind)


def setup_inputs(seed: int = 0) -> dict:
    streams_of = jax.random.split(jax.random.key(seed), 8)
    up_tiles = gaussian(streams_of[0], (LEVELS, KT, TILE, TILE), (KT * TILE // NT) ** -0.5, 0.3125, ((0, 256),))
    up_at = draw_up_at(jax.random.fold_in(streams_of[7], 71), 0)
    down_tiles = gaussian(streams_of[2], (LEVELS, KT, TILE, TILE), (KT * TILE // NT) ** -0.5, 0.3125, ((0, 256),))
    down_at = draw_down_at(jax.random.fold_in(streams_of[7], 71), 0)
    diag_tiles = gaussian(streams_of[4], (PAIRS, KT, TILE, TILE), 1.0, 6.0, ((0, 256),))
    diag_at = draw_diag_at(jax.random.fold_in(streams_of[7], 71), 0)
    odd_inverse = gaussian(streams_of[6], (PAIRS, P_SIZE, P_SIZE), 1.0, 6.0, ((0, 256),))
    return {"up_tiles": up_tiles, "up_at": up_at, "down_tiles": down_tiles, "down_at": down_at, "diag_tiles": diag_tiles, "diag_at": diag_at, "odd_inverse": odd_inverse}


def expand_tiles(tiles, places):
    onehot = (places[None, :] == jnp.arange(NT * NT, dtype=jnp.int32)[:, None]).astype(jnp.float32)
    blocks = jnp.einsum('pk,kij->pij', onehot, tiles.astype(jnp.float32), precision=lax.Precision.HIGHEST)
    return blocks.reshape(NT, NT, TILE, TILE).transpose(0, 2, 1, 3).reshape(P_SIZE, P_SIZE)


def left_sparse(tiles, places, dense):
    width = dense.shape[1]
    tile_rows = (places // NT).astype(jnp.int32)
    tile_cols = (places % NT).astype(jnp.int32)
    picked = jnp.take(dense.reshape(NT, TILE, width), tile_cols, axis=0)
    parts = jnp.einsum('kij,kjn->kin', tiles.astype(jnp.float32), picked.astype(jnp.float32), precision=lax.Precision.HIGHEST)
    onehot = (tile_rows[None, :] == jnp.arange(NT, dtype=jnp.int32)[:, None]).astype(jnp.float32)
    summed = jnp.einsum('rk,kin->rin', onehot, parts, precision=lax.Precision.HIGHEST)
    return summed.reshape(P_SIZE, width)


def right_sparse(dense, tiles, places):
    height = dense.shape[0]
    tile_rows = (places // NT).astype(jnp.int32)
    tile_cols = (places % NT).astype(jnp.int32)
    picked = jnp.take(dense.reshape(height, NT, TILE), tile_rows, axis=1)
    parts = jnp.einsum('mki,kij->kmj', picked.astype(jnp.float32), tiles.astype(jnp.float32), precision=lax.Precision.HIGHEST)
    onehot = (tile_cols[None, :] == jnp.arange(NT, dtype=jnp.int32)[:, None]).astype(jnp.float32)
    summed = jnp.einsum('ck,kmj->mcj', onehot, parts, precision=lax.Precision.HIGHEST)
    return summed.reshape(height, P_SIZE)


def odd_products(inverse, up_block, up_places, down_block, down_places):
    first = right_sparse(inverse, up_block, up_places)
    second = right_sparse(inverse, down_block, down_places)
    return jnp.stack([first, second]).astype(jnp.bfloat16)


def reference(up_tiles, up_at, down_tiles, down_at, diag_tiles, diag_at, odd_inverse):
    inputs = (up_tiles[0::2], up_at[0::2], up_tiles[1::2], up_at[1::2],
              down_tiles[0::2], down_at[0::2], down_tiles[1::2], down_at[1::2],
              diag_tiles, diag_at, odd_inverse, jnp.arange(PAIRS, dtype=jnp.int32))

    def advance(previous, pieces):
        (even_up, even_up_at, odd_up, odd_up_at, even_down, even_down_at,
         odd_down, odd_down_at, diagonal, diag_places, inverse, level) = pieces
        current = odd_products(inverse, odd_up, odd_up_at, odd_down, odd_down_at)
        up_low = left_sparse(even_up, even_up_at, current[0])
        up_high = left_sparse(even_up, even_up_at, current[1])
        below_low = left_sparse(even_down, even_down_at, previous[0])
        below_high = left_sparse(even_down, even_down_at, previous[1])
        new_up = (-up_low).astype(jnp.bfloat16)
        new_down = (-below_high).astype(jnp.bfloat16)
        new_diag = (expand_tiles(diagonal, diag_places) - up_high - below_low).astype(jnp.bfloat16)
        weight = (PAIRS + 2 * level).astype(jnp.float32) / PAIRS
        term = weight * jnp.mean(new_up.astype(jnp.float32), axis=0)
        return current, (new_diag, new_up, new_down, term)

    start = jnp.zeros((2, P_SIZE, P_SIZE), jnp.bfloat16)
    _, outputs = lax.scan(advance, start, inputs)
    new_diag, new_up, new_down, terms = outputs
    return new_diag, new_up, new_down, jnp.cumsum(terms, axis=0)
```

```python
import functools

import jax
import jax.numpy as jnp
from jax import lax
from jax.experimental import pallas as pl
from jax.experimental.pallas import tpu as pltpu
from jax.sharding import PartitionSpec as P

TILE = 128
NT = 8
P_SIZE = 1024
KT = 24
WIDE = 256
AXES = ("grp", "lev")
MESH = pl.DeviceIdType.MESH
F32 = jnp.float32
BF16 = jnp.bfloat16


def vmem():
    return pl.BlockSpec(memory_space=pltpu.VMEM)


def smem():
    return pl.BlockSpec(memory_space=pltpu.SMEM)


def expand(dense, tiles, at, row, tile_row=None):
    dense[...] = jnp.zeros_like(dense)

    def place(k, carry):
        p = at[row, k]
        r = pl.multiple_of((p // NT) * TILE, TILE)
        c = pl.multiple_of((p % NT) * TILE, TILE)
        tile = tiles[k] if tile_row is None else tiles[tile_row, k]
        dense[pl.ds(r, TILE), pl.ds(c, TILE)] = tile
        return carry

    lax.fori_loop(0, KT, place, 0, unroll=4)


def column_blocks(body):
    def step(b, carry):
        body(pl.ds(pl.multiple_of(b * WIDE, WIDE), WIDE))
        return carry

    lax.fori_loop(0, P_SIZE // WIDE, step, 0)


def mm(a, b):
    return jnp.dot(a, b, preferred_element_type=F32)


def own_kernel(
    up_at, down_at, diag_at, up, down, diag, inv, new_up, rest, term, wide, prod, even
):
    level = lax.axis_index("grp") * lax.axis_size("lev") + lax.axis_index("lev")
    count = lax.axis_size("grp") * lax.axis_size("lev")
    weight = (count + 2 * level).astype(F32) / count
    expand(wide, up, up_at, 1, 1)

    def first(cols):
        prod[:, cols] = mm(inv[0], wide[:, cols]).astype(BF16)

    column_blocks(first)
    expand(even, up, up_at, 0, 0)

    def second(cols):
        out = (-mm(even[...], prod[:, cols])).astype(BF16)
        new_up[0, :, cols] = out
        mean = jnp.sum(out.astype(F32), axis=0, keepdims=True) / P_SIZE
        term[:, cols] = weight * mean

    column_blocks(second)
    expand(wide, down, down_at, 1, 1)
    column_blocks(first)
    expand(wide, diag, diag_at, 0, 0)

    def third(cols):
        rest[:, cols] = wide[:, cols].astype(F32) - mm(even[...], prod[:, cols])

    column_blocks(third)


def own_products(up_at, down_at, diag_at, up, down, diag, inv):
    return pl.pallas_call(
        own_kernel,
        name="own_products",
        out_shape=(
            jax.ShapeDtypeStruct((1, P_SIZE, P_SIZE), BF16),
            jax.ShapeDtypeStruct((P_SIZE, P_SIZE), F32),
            jax.ShapeDtypeStruct((1, P_SIZE), F32),
        ),
        in_specs=[smem()] * 3 + [vmem()] * 4,
        out_specs=(vmem(),) * 3,
        scratch_shapes=[pltpu.VMEM((P_SIZE, P_SIZE), BF16)] * 3,
        compiler_params=pltpu.CompilerParams(vmem_limit_bytes=32 << 20),
        cost_estimate=pl.CostEstimate(
            flops=4 * 2 * P_SIZE**3, bytes_accessed=12 << 20, transcendentals=0
        ),
    )(up_at, down_at, diag_at, up, down, diag, inv)


def scan_kernel(bits, term, out, total, incoming, send_sem, recv_sem):
    inner = lax.axis_size("lev")
    me = lax.axis_index("grp") * inner + lax.axis_index("lev")
    partners, upper = [], []
    for d in range(bits):
        bit = (me // 2**d) % 2
        other = me + 2**d * (1 - 2 * bit)
        upper.append(bit)
        partners.append((other // inner, other % inner))
    barrier = pltpu.get_barrier_semaphore()
    for p in partners:
        pl.semaphore_signal(barrier, inc=1, device_id=p, device_id_type=MESH)
    pl.semaphore_wait(barrier, bits)
    out[...] = term[...]
    total[0] = term[...]
    for d in range(bits):
        copy = pltpu.make_async_remote_copy(
            src_ref=total.at[d],
            dst_ref=incoming.at[d],
            send_sem=send_sem.at[d],
            recv_sem=recv_sem.at[d],
            device_id=partners[d],
            device_id_type=MESH,
        )
        copy.start()
        copy.wait()
        got = incoming[d]
        out[...] += got * upper[d].astype(F32)
        if d < bits - 1:
            total[d + 1] = total[d] + got


def scan_terms(term, count):
    bits = count.bit_length() - 1
    return pl.pallas_call(
        functools.partial(scan_kernel, bits),
        name="scan_terms",
        out_shape=jax.ShapeDtypeStruct((1, P_SIZE), F32),
        in_specs=[vmem()],
        out_specs=vmem(),
        scratch_shapes=[
            pltpu.VMEM((bits, 1, P_SIZE), F32),
            pltpu.VMEM((bits, 1, P_SIZE), F32),
            pltpu.SemaphoreType.DMA((bits,)),
            pltpu.SemaphoreType.DMA((bits,)),
        ],
        compiler_params=pltpu.CompilerParams(
            collective_id=0, has_side_effects=True, vmem_limit_bytes=4 << 20
        ),
    )(term)


def left_kernel(at, tiles, inv, out, even):
    expand(even, tiles, at, 0, 0)

    def step(cols):
        out[:, cols] = mm(even[...], inv[0, :, cols]).astype(BF16)

    column_blocks(step)


def left_product(down_at, down, inv):
    return pl.pallas_call(
        left_kernel,
        name="left_product",
        out_shape=jax.ShapeDtypeStruct((P_SIZE, P_SIZE), BF16),
        in_specs=[smem(), vmem(), vmem()],
        out_specs=vmem(),
        scratch_shapes=[pltpu.VMEM((P_SIZE, P_SIZE), BF16)],
        compiler_params=pltpu.CompilerParams(vmem_limit_bytes=16 << 20),
        cost_estimate=pl.CostEstimate(
            flops=2 * P_SIZE**3, bytes_accessed=5 << 20, transcendentals=0
        ),
    )(down_at, down, inv)


def diag_kernel(at, left, tiles, rest, out, wide):
    expand(wide, tiles, at, 0)

    def step(cols):
        out[0, :, cols] = (rest[:, cols] - mm(left[...], wide[:, cols])).astype(BF16)

    column_blocks(step)


def down_kernel(at, left, tiles, out, wide):
    expand(wide, tiles, at, 1)

    def step(cols):
        out[0, :, cols] = (-mm(left[...], wide[:, cols])).astype(BF16)

    column_blocks(step)


def right_product(kernel, name, at, *operands):
    return pl.pallas_call(
        kernel,
        name=name,
        out_shape=jax.ShapeDtypeStruct((1, P_SIZE, P_SIZE), BF16),
        in_specs=[smem()] + [vmem()] * len(operands),
        out_specs=vmem(),
        scratch_shapes=[pltpu.VMEM((P_SIZE, P_SIZE), BF16)],
        compiler_params=pltpu.CompilerParams(vmem_limit_bytes=16 << 20),
        cost_estimate=pl.CostEstimate(
            flops=2 * P_SIZE**3, bytes_accessed=5 << 20, transcendentals=0
        ),
    )(at, *operands)


def local(count, up_tiles, up_at, down_tiles, down_at, diag_tiles, diag_at, odd_inverse):
    route = [(i, i + 1) for i in range(count - 1)]

    def passed(block):
        return lax.ppermute(block, AXES, route)

    inv_below = passed(odd_inverse)
    at_below = passed(jnp.stack([up_at[1], down_at[1]]))
    up_below = passed(up_tiles[1])
    down_below = passed(down_tiles[1])
    new_up, rest, term = own_products(
        up_at, down_at, diag_at, up_tiles, down_tiles, diag_tiles, odd_inverse
    )
    sums = scan_terms(term, count)
    left = left_product(down_at, down_tiles, inv_below)
    new_diag = right_product(diag_kernel, "diag", at_below, left, up_below, rest)
    new_down = right_product(down_kernel, "down", at_below, left, down_below)
    return new_diag, new_up, new_down, sums


def solution(mesh):
    count = mesh.shape["grp"] * mesh.shape["lev"]
    return jax.shard_map(
        functools.partial(local, count),
        mesh=mesh,
        in_specs=(
            P(AXES, None, None, None),
            P(AXES, None),
            P(AXES, None, None, None),
            P(AXES, None),
            P(AXES, None, None, None),
            P(AXES, None),
            P(AXES, None, None),
        ),
        out_specs=(
            P(AXES, None, None),
            P(AXES, None, None),
            P(AXES, None, None),
            P(AXES, None),
        ),
        check_vma=False,
    )
```

```python
import functools

import jax
import jax.numpy as jnp
from jax import lax
from jax.experimental import pallas as pl
from jax.experimental.pallas import tpu as pltpu
from jax.sharding import PartitionSpec as P

TILE = 128
NT = 8
P_SIZE = 1024
KT = 24
HALF = KT // 2
WIDE = 256
RADIX = 4
AXES = ("grp", "lev")
MESH = pl.DeviceIdType.MESH
F32 = jnp.float32
BF16 = jnp.bfloat16
I32 = jnp.int32
INV, UP, PLACE, DOWN_A, DOWN_B, HOP_1, HOP_2, HOP_3, SCAN = range(9)


def mm(a, b):
    return jnp.dot(a, b, preferred_element_type=F32)


def column_blocks(body):
    def step(b, carry):
        body(pl.ds(pl.multiple_of(b * WIDE, WIDE), WIDE))
        return carry

    lax.fori_loop(0, P_SIZE // WIDE, step, 0)


def expand(dense, tile_of, slots, row):
    def tile_row(r, carry):
        rows = pl.ds(pl.multiple_of(r * TILE, TILE), TILE)
        for c in range(NT):
            slot = slots[row, r * NT + c]
            tile = tile_of(jnp.clip(slot, 0, KT - 1))
            dense[rows, c * TILE : (c + 1) * TILE] = jnp.where(slot >= 0, tile, jnp.zeros_like(tile))
        return carry

    lax.fori_loop(0, NT, tile_row, 0)


def slot_row(places):
    number = lax.broadcasted_iota(I32, (KT, KT), 0)
    lane = lax.broadcasted_iota(I32, (KT, KT), 1)
    spread = jnp.broadcast_to(places, (KT, KT))
    column = jnp.sum(jnp.where(number == lane, spread, 0), axis=1, keepdims=True)
    position = lax.broadcasted_iota(I32, (KT, TILE), 1)
    index = lax.broadcasted_iota(I32, (KT, TILE), 0) + 1
    hit = jnp.broadcast_to(column, (KT, TILE)) == position
    return jnp.max(jnp.where(hit, index, 0), axis=0, keepdims=True) - 1


def exchange_kernel(
    sizes,
    up_at,
    down_at,
    diag_at,
    up,
    down,
    diag,
    inv,
    left,
    down_in,
    places_in,
    new_up,
    new_diag,
    sums,
    up_at_v,
    down_at_v,
    diag_at_v,
    up_v,
    down_v,
    diag_v,
    inv_v,
    places,
    slots,
    slots_in,
    inv_in,
    up_in,
    hop_1,
    hop_2,
    wide,
    even,
    prod,
    rest,
    total,
    incoming,
    local_sem,
    send_sem,
    recv_sem,
):
    groups, inner, length = sizes
    count = groups * inner
    lev = lax.axis_index("lev")
    grp = lax.axis_index("grp")
    me = grp * inner + lev
    core = lev % 2

    def at(index):
        index = (index + count) % count
        return (index // inner, index % inner)

    def along(distance):
        z = (lev // 2) % length
        return (grp, lev - 2 * z + 2 * ((z + distance + length) % length))

    following, before = at(me + 1), at(me - 1)
    behind, ahead = along(-3), along(3)
    origin_g, origin_l = along(-2)
    target = at(origin_g * inner + origin_l + 1)
    prev_g, prev_l = before
    prev_z = (prev_l // 2) % length
    holder = (prev_g, prev_l - 2 * prev_z + 2 * ((prev_z + 2) % length))
    third_g = core * target[0] + (1 - core) * holder[0]
    third_l = core * target[1] + (1 - core) * holder[1]

    peers = [following, before, behind, ahead, (third_g, third_l)]
    rounds = []
    stride = 1
    while stride < count:
        digit = (me // stride) % RADIX
        others = [
            at(me - digit * stride + ((digit + j) % RADIX) * stride) for j in range(1, RADIX)
        ]
        rounds.append((digit, others))
        peers += others
        stride *= RADIX

    def load(source, target, sem):
        copy = pltpu.make_async_copy(source, target, local_sem.at[sem])
        copy.start()
        return copy

    load_up_at = load(up_at, up_at_v, 0)
    load_down_at = load(down_at, down_at_v, 1)
    load_diag_at = load(diag_at, diag_at_v, 2)
    load_up = load(up, up_v, 3)
    load_inv = load(inv.at[0], inv_v, 4)
    load_down = load(down, down_v, 5)
    load_diag = load(diag.at[0], diag_v, 6)

    barrier = pltpu.get_barrier_semaphore()
    for p in peers:
        pl.semaphore_signal(barrier, inc=1, device_id=p, device_id_type=MESH)
    pl.semaphore_wait(barrier, len(peers))

    def remote(source, target, send, recv, device):
        return pltpu.make_async_remote_copy(
            src_ref=source,
            dst_ref=target,
            send_sem=send_sem.at[send],
            recv_sem=recv_sem.at[recv],
            device_id=device,
            device_id_type=MESH,
        )

    first_half, second_half = pl.ds(0, HALF), pl.ds(HALF, HALF)
    send_hop_1 = remote(down.at[1, second_half], hop_1, HOP_1, HOP_1, behind)
    send_hop_2 = remote(hop_1, hop_2, HOP_2, HOP_2, behind)
    send_hop_3 = remote(hop_2, down_in.at[second_half], HOP_3, DOWN_B, target)
    send_down_b = remote(
        down.at[1, second_half], down_in.at[second_half], DOWN_B, DOWN_B, following
    )
    send_inv = remote(inv.at[0], inv_in, INV, INV, following)
    send_up = remote(up.at[1], up_in, UP, UP, following)
    send_places = remote(places, places_in, PLACE, PLACE, following)
    send_down_a = remote(
        down.at[1, first_half], down_in.at[first_half], DOWN_A, DOWN_A, following
    )

    @pl.when(core == 1)
    def _():
        send_hop_1.start()

    send_inv.start()
    send_up.start()
    load_up_at.wait()
    load_down_at.wait()
    load_diag_at.wait()
    places[...] = jnp.full_like(places, -1)
    places[0:1] = slot_row(up_at_v[1:2])
    places[1:2] = slot_row(down_at_v[1:2])
    places[2:3] = slot_row(up_at_v[0:1])
    places[3:4] = slot_row(down_at_v[0:1])
    places[4:5] = slot_row(diag_at_v[...])
    send_places.start()
    send_down_a.start()

    @pl.when(core == 0)
    def _():
        send_down_b.start()

    load_slots = load(places, slots, 7)
    load_slots.wait()
    load_up.wait()
    expand(wide, lambda s: up_v[1, s], slots, 0)
    load_inv.wait()

    def odd_product(cols):
        prod[:, cols] = mm(inv_v[...], wide[:, cols]).astype(BF16)

    column_blocks(odd_product)
    expand(even, lambda s: up_v[0, s], slots, 2)
    weight = (count + 2 * me).astype(F32) / count

    def up_product(cols):
        out = (-mm(even[...], prod[:, cols])).astype(BF16)
        new_up[:, cols] = out
        mean = jnp.sum(out.astype(F32), axis=0, keepdims=True) / P_SIZE
        total[0, :, cols] = weight * mean

    column_blocks(up_product)

    def scan_copies(n):
        return [
            remote(
                total.at[n],
                incoming.at[3 * n + j],
                SCAN + 3 * n + j,
                SCAN + 3 * n + j,
                rounds[n][1][j],
            )
            for j in range(RADIX - 1)
        ]

    def scan_start(n):
        for copy in scan_copies(n):
            copy.start()

    def scan_finish(n):
        for copy in scan_copies(n):
            copy.wait()
        digit = rounds[n][0]
        so_far = total[n]
        for j in range(RADIX - 1):
            got = incoming[3 * n + j]
            so_far = so_far + got
            sums[...] += jnp.where(digit > j, got, jnp.zeros_like(got))
        if n < len(rounds) - 1:
            total[n + 1] = so_far

    sums[...] = total[0]
    scan_start(0)
    load_down.wait()
    expand(wide, lambda s: down_v[1, s], slots, 1)
    column_blocks(odd_product)
    scan_finish(0)
    scan_start(1)
    load_diag.wait()
    expand(wide, lambda s: diag_v[s], slots, 4)

    def rest_product(cols):
        rest[:, cols] = wide[:, cols].astype(F32) - mm(even[...], prod[:, cols])

    column_blocks(rest_product)
    scan_finish(1)
    scan_start(2)
    expand(even, lambda s: down_v[0, s], slots, 3)

    @pl.when(core == 1)
    def _():
        send_hop_1.wait()
        send_hop_2.start()

    scan_finish(2)
    scan_start(3)
    send_inv.wait()

    def left_product(cols):
        out = mm(even[...], inv_in[:, cols])
        left[:, cols] = jnp.where(me > 0, out, jnp.zeros_like(out)).astype(BF16)

    column_blocks(left_product)

    @pl.when(core == 1)
    def _():
        send_hop_2.wait()
        send_hop_3.start()

    scan_finish(3)
    send_places.wait()
    load_slots_in = load(places_in, slots_in, 8)
    load_slots_in.wait()
    send_up.wait()
    expand(wide, lambda s: up_in[s], slots_in, 0)

    def diag_product(cols):
        new_diag[:, cols] = (rest[:, cols] - mm(left[...], wide[:, cols])).astype(BF16)

    column_blocks(diag_product)
    send_down_a.wait()

    @pl.when(core == 1)
    def _():
        send_hop_3.wait_send()

    @pl.when(core == 0)
    def _():
        send_down_b.wait_send()

    send_down_b.wait_recv()


def exchange(sizes, *operands):
    dense = pltpu.VMEM((P_SIZE, P_SIZE), BF16)
    rounds = (sizes[0] * sizes[1]).bit_length() // 2
    vmem = pl.BlockSpec(memory_space=pltpu.VMEM)
    square = jax.ShapeDtypeStruct((P_SIZE, P_SIZE), BF16)
    return pl.pallas_call(
        functools.partial(exchange_kernel, sizes),
        name="exchange",
        out_shape=(
            square,
            jax.ShapeDtypeStruct((KT, TILE, TILE), BF16),
            jax.ShapeDtypeStruct((NT, TILE), I32),
            square,
            square,
            jax.ShapeDtypeStruct((1, P_SIZE), F32),
        ),
        in_specs=[pl.BlockSpec(memory_space=pltpu.HBM)] * 7,
        out_specs=(vmem,) * 6,
        scratch_shapes=[
            pltpu.VMEM((2, KT), I32),
            pltpu.VMEM((2, KT), I32),
            pltpu.VMEM((1, KT), I32),
            pltpu.VMEM((2, KT, TILE, TILE), BF16),
            pltpu.VMEM((2, KT, TILE, TILE), BF16),
            pltpu.VMEM((KT, TILE, TILE), BF16),
            dense,
            pltpu.VMEM((NT, TILE), I32),
            pltpu.SMEM((NT, TILE), I32),
            pltpu.SMEM((NT, TILE), I32),
            dense,
            pltpu.VMEM((KT, TILE, TILE), BF16),
            pltpu.VMEM((HALF, TILE, TILE), BF16),
            pltpu.VMEM((HALF, TILE, TILE), BF16),
            dense,
            dense,
            dense,
            pltpu.VMEM((P_SIZE, P_SIZE), F32),
            pltpu.VMEM((rounds, 1, P_SIZE), F32),
            pltpu.VMEM((3 * rounds, 1, P_SIZE), F32),
            pltpu.SemaphoreType.DMA((9,)),
            pltpu.SemaphoreType.DMA((SCAN + 3 * rounds,)),
            pltpu.SemaphoreType.DMA((SCAN + 3 * rounds,)),
        ],
        compiler_params=pltpu.CompilerParams(
            collective_id=0, has_side_effects=True, vmem_limit_bytes=54 << 20
        ),
    )(*operands)


def finish_kernel(
    places, left, tiles, up_in, diag_in, sums_in, new_diag, new_up, new_down, sums, wide, out, sem
):
    copies = [
        pltpu.make_async_copy(up_in, new_up.at[0], sem.at[0]),
        pltpu.make_async_copy(diag_in, new_diag.at[0], sem.at[1]),
    ]
    for copy in copies:
        copy.start()
    sums[...] = sums_in[...]
    expand(wide, lambda s: tiles[s], places, 1)
    for b in range(P_SIZE // WIDE):
        cols = pl.ds(b * WIDE, WIDE)
        out[:, cols] = (-mm(left[...], wide[:, cols])).astype(BF16)
        copy = pltpu.make_async_copy(out.at[:, cols], new_down.at[0, :, cols], sem.at[2 + b])
        copy.start()
        copies.append(copy)
    for copy in copies:
        copy.wait()


def finish(places, *operands):
    vmem = pl.BlockSpec(memory_space=pltpu.VMEM)
    hbm = pl.BlockSpec(memory_space=pltpu.HBM)
    square = jax.ShapeDtypeStruct((1, P_SIZE, P_SIZE), BF16)
    return pl.pallas_call(
        finish_kernel,
        name="finish",
        out_shape=(square, square, square, jax.ShapeDtypeStruct((1, P_SIZE), F32)),
        in_specs=[pl.BlockSpec(memory_space=pltpu.SMEM)] + [vmem] * 5,
        out_specs=(hbm, hbm, hbm, vmem),
        scratch_shapes=[
            pltpu.VMEM((P_SIZE, P_SIZE), BF16),
            pltpu.VMEM((P_SIZE, P_SIZE), BF16),
            pltpu.SemaphoreType.DMA((2 + P_SIZE // WIDE,)),
        ],
        compiler_params=pltpu.CompilerParams(vmem_limit_bytes=16 << 20),
    )(places, *operands)


def local(sizes, up_tiles, up_at, down_tiles, down_at, diag_tiles, diag_at, odd_inverse):
    left, down_in, places_in, new_up, new_diag, sums = exchange(
        sizes, up_at, down_at, diag_at, up_tiles, down_tiles, diag_tiles, odd_inverse
    )
    return finish(places_in, left, down_in, new_up, new_diag, sums)


def solution(mesh):
    sizes = (mesh.shape["grp"], mesh.shape["lev"], 8)
    return jax.shard_map(
        functools.partial(local, sizes),
        mesh=mesh,
        in_specs=(
            P(AXES, None, None, None),
            P(AXES, None),
            P(AXES, None, None, None),
            P(AXES, None),
            P(AXES, None, None, None),
            P(AXES, None),
            P(AXES, None, None),
        ),
        out_specs=(
            P(AXES, None, None),
            P(AXES, None, None),
            P(AXES, None, None),
            P(AXES, None),
        ),
        check_vma=False,
    )
```

```python
import functools

import jax
import jax.numpy as jnp
from jax import lax
from jax.experimental import pallas as pl
from jax.experimental.pallas import tpu as pltpu
from jax.sharding import PartitionSpec as P

TILE = 128
NT = 8
P_SIZE = 1024
KT = 24
HALF = KT // 2
WIDE = 256
DEPTH = 8
SIDE = 4
STEPS = (1, 2, 4)
AXES = ("grp", "lev")
MESH = pl.DeviceIdType.MESH
F32 = jnp.float32
BF16 = jnp.bfloat16
I32 = jnp.int32
INV, UP, PLACE, DOWN, HOP, PAIR, LINE, COLUMN = 0, 1, 2, 3, 5, 7, 8, 14


def mm(a, b):
    return jnp.dot(a, b, preferred_element_type=F32)


def column_blocks(body):
    def step(b, carry):
        body(pl.ds(pl.multiple_of(b * WIDE, WIDE), WIDE))
        return carry

    lax.fori_loop(0, P_SIZE // WIDE, step, 0)


def expand(dense, tile_of, slots, row, below=KT):
    def tile_row(r, carry):
        rows = pl.ds(pl.multiple_of(r * TILE, TILE), TILE)
        for c in range(NT):
            slot = slots[row, r * NT + c]
            tile = tile_of(jnp.clip(slot, 0, below - 1))
            here = (slot >= 0) & (slot < below)
            dense[rows, c * TILE : (c + 1) * TILE] = jnp.where(here, tile, jnp.zeros_like(tile))
        return carry

    lax.fori_loop(0, NT, tile_row, 0)


def slot_row(places):
    number = lax.broadcasted_iota(I32, (KT, KT), 0)
    lane = lax.broadcasted_iota(I32, (KT, KT), 1)
    spread = jnp.broadcast_to(places, (KT, KT))
    column = jnp.sum(jnp.where(number == lane, spread, 0), axis=1, keepdims=True)
    position = lax.broadcasted_iota(I32, (KT, TILE), 1)
    index = lax.broadcasted_iota(I32, (KT, TILE), 0) + 1
    hit = jnp.broadcast_to(column, (KT, TILE)) == position
    return jnp.max(jnp.where(hit, index, 0), axis=0, keepdims=True) - 1


def exchange_kernel(
    sizes,
    up_at,
    down_at,
    diag_at,
    up,
    down,
    diag,
    inv,
    left,
    down_wide,
    down_in,
    places_in,
    new_up,
    new_diag,
    sums,
    up_at_v,
    down_at_v,
    diag_at_v,
    up_v,
    down_v,
    diag_v,
    inv_v,
    places,
    slots,
    slots_in,
    inv_in,
    up_in,
    first_in,
    hop,
    wide,
    even,
    prod,
    rest,
    term,
    pair,
    pair_in,
    columns_in,
    rising,
    falling,
    rising_in,
    falling_in,
    local_sem,
    send_sem,
    recv_sem,
    near_sem,
    far_sem,
):
    groups, inner = sizes
    count = groups * inner
    lev = lax.axis_index("lev")
    grp = lax.axis_index("grp")
    me = grp * inner + lev
    core = lev % 2
    z = (lev // 2) % DEPTH
    column = me // (2 * DEPTH)
    columns = count // (2 * DEPTH)

    def place_of(index):
        return (index // inner, index % inner)

    def up_line(distance):
        return place_of(me + 2 * distance)

    other_core = place_of(me + 1 - 2 * core)
    same_z = [
        place_of(((column + j) % columns) * 2 * DEPTH + 2 * z + core) for j in range(1, columns)
    ]
    has_next, has_prev = me < count - 1, me > 0
    inside = column < columns - 1
    far_end = (core == 1) & (z == 7) & inside
    second = (core == 1) & (z == 4) & inside
    third = (core == 1) & (z == 1) & inside
    hop_from = (core == 0) & (z == 0) & has_prev
    target = place_of((column + 1) * 2 * DEPTH)
    holder = place_of((column - 1) * 2 * DEPTH + 3)

    def load(source, target, sem):
        copy = pltpu.make_async_copy(source, target, local_sem.at[sem])
        copy.start()
        return copy

    barrier = pltpu.get_barrier_semaphore()

    def tell(device):
        pl.semaphore_signal(barrier, inc=1, device_id=device, device_id_type=MESH)

    def tell_if(condition, device):
        @pl.when(condition)
        def _():
            tell(device)

    tell_if(has_prev, place_of(me - 1))
    tell(other_core)
    tell_if(z >= 1, up_line(-1))
    for step in STEPS:
        tell_if(z + step < DEPTH, up_line(step))
    tell_if(second | third, up_line(3))
    tell_if(hop_from, holder)
    for device in same_z:
        tell(device)

    load_up_at = load(up_at, up_at_v, 0)
    load_down_at = load(down_at, down_at_v, 1)
    load_diag_at = load(diag_at, diag_at_v, 2)
    load_up = load(up, up_v, 3)
    load_inv = load(inv.at[0], inv_v, 4)
    load_down = load(down, down_v, 5)
    load_diag = load(diag.at[0], diag_v, 6)

    expected = len(same_z) + 1
    for condition in (has_next, z < DEPTH - 1, z >= 1, z >= 2, z >= 4, far_end, second, third):
        expected += condition.astype(I32)
    pl.semaphore_wait(barrier, expected)

    def remote(source, target, send, recv, device):
        return pltpu.make_async_remote_copy(
            src_ref=source,
            dst_ref=target,
            send_sem=send_sem.at[send],
            recv_sem=recv_sem.at[recv],
            device_id=device,
            device_id_type=MESH,
        )

    halves = [pl.ds(c * HALF, HALF) for c in range(2)]
    following = place_of(me + 1)
    send_inv = remote(inv.at[0], inv_in, INV, INV, following)
    send_up = remote(up.at[1], up_in, UP, UP, following)
    send_places = remote(places, places_in, PLACE, PLACE, following)
    send_down = [
        remote(down.at[1, h], landing, DOWN + c, DOWN + c, following)
        for c, (h, landing) in enumerate(zip(halves, (first_in, down_in)))
    ]
    send_back = [
        remote(down.at[1, h], hop.at[h], HOP + c, HOP + c, up_line(-3))
        for c, h in enumerate(halves)
    ]
    send_on = [
        remote(hop.at[h], hop.at[h], HOP + c, HOP + c, up_line(-3)) for c, h in enumerate(halves)
    ]
    send_home = [
        remote(hop.at[h], landing, HOP + c, DOWN + c, target)
        for c, (h, landing) in enumerate(zip(halves, (first_in, down_in)))
    ]

    @pl.when(far_end)
    def _():
        for copy in send_back:
            copy.start()

    @pl.when(has_next)
    def _():
        send_inv.start()
        send_up.start()

    load_up_at.wait()
    load_down_at.wait()
    load_diag_at.wait()
    places[...] = jnp.full_like(places, -1)
    places[0:1] = slot_row(up_at_v[1:2])
    places[1:2] = slot_row(down_at_v[1:2])
    places[2:3] = slot_row(up_at_v[0:1])
    places[3:4] = slot_row(down_at_v[0:1])
    places[4:5] = slot_row(diag_at_v[...])
    places[5:6, 0:KT] = down_at_v[1:2]

    @pl.when(has_next)
    def _():
        send_places.start()

    @pl.when(has_next & ~far_end)
    def _():
        for copy in send_down:
            copy.start()

    @pl.when(z >= 1)
    def _():
        pl.semaphore_signal(near_sem, inc=1, device_id=up_line(-1), device_id_type=MESH)

    @pl.when(me == 0)
    def _():
        inv_in[...] = jnp.zeros_like(inv_in)
        up_in[...] = jnp.zeros_like(up_in)
        first_in[...] = jnp.zeros_like(first_in)
        down_in[...] = jnp.zeros_like(down_in)
        places_in[...] = jnp.zeros_like(places_in)

    load_slots = load(places, slots, 7)
    load_slots.wait()
    load_up.wait()
    expand(wide, lambda s: up_v[1, s], slots, 0)
    load_inv.wait()

    def odd_product(cols):
        prod[:, cols] = mm(inv_v[...], wide[:, cols]).astype(BF16)

    column_blocks(odd_product)

    @pl.when(z < DEPTH - 1)
    def _():
        pl.semaphore_wait(near_sem, 1)

    @pl.when(z >= 2)
    def _():
        pl.semaphore_signal(far_sem, inc=1, device_id=up_line(-2), device_id_type=MESH)

    expand(even, lambda s: up_v[0, s], slots, 2)
    weight = (count + 2 * me).astype(F32) / count

    def up_product(cols):
        out = (-mm(even[...], prod[:, cols])).astype(BF16)
        new_up[:, cols] = out
        mean = jnp.sum(out.astype(F32), axis=0, keepdims=True) / P_SIZE
        term[:, cols] = weight * mean

    column_blocks(up_product)

    send_term = remote(term, pair_in, PAIR, PAIR, other_core)
    send_term.start()
    load_down.wait()
    expand(wide, lambda s: down_v[1, s], slots, 1)
    send_term.wait()
    pair[...] = term[...] + pair_in[...]
    sums[...] = term[...] + jnp.where(core == 1, pair_in[...], jnp.zeros_like(term))
    send_pair = [
        remote(pair, columns_in.at[j], COLUMN + j, COLUMN + j, device)
        for j, device in enumerate(same_z)
    ]
    for copy in send_pair:
        copy.start()
    column_blocks(odd_product)

    @pl.when(z < DEPTH - 2)
    def _():
        pl.semaphore_wait(far_sem, 1)

    load_diag.wait()
    expand(wide, lambda s: diag_v[s], slots, 4)

    def rest_product(cols):
        rest[:, cols] = wide[:, cols].astype(F32) - mm(even[...], prod[:, cols])

    column_blocks(rest_product)
    for copy in send_pair:
        copy.wait()
    lower = jnp.zeros_like(term)
    for j in range(columns - 1):
        got = columns_in[j]
        lower += jnp.where(column > j, got, jnp.zeros_like(got))
    sums[...] += lower
    rising[0] = lower + pair[...]
    falling[0] = lower

    def line_copies(n):
        up_step = remote(
            rising.at[n], rising_in.at[n], LINE + 2 * n, LINE + 2 * n, up_line(STEPS[n])
        )
        down_step = remote(
            falling.at[n],
            falling_in.at[n],
            LINE + 2 * n + 1,
            LINE + 2 * n + 1,
            up_line(-STEPS[n]),
        )
        return up_step, down_step

    def line_start(n):
        up_step, down_step = line_copies(n)

        @pl.when(z + STEPS[n] < DEPTH)
        def _():
            up_step.start()

        @pl.when(z >= STEPS[n])
        def _():
            down_step.start()

    def line_finish(n):
        up_step, down_step = line_copies(n)
        last = n == len(STEPS) - 1
        if not last:
            rising[n + 1] = rising[n]
            falling[n + 1] = falling[n]

        @pl.when(z >= STEPS[n])
        def _():
            down_step.wait_send()
            up_step.wait_recv()
            sums[...] += rising_in[n]
            if not last:
                rising[n + 1] += rising_in[n]

        @pl.when(z + STEPS[n] < DEPTH)
        def _():
            up_step.wait_send()
            down_step.wait_recv()
            sums[...] += falling_in[n]
            if not last:
                falling[n + 1] += falling_in[n]

    line_start(0)
    expand(even, lambda s: down_v[0, s], slots, 3)

    @pl.when(second)
    def _():
        for arrived, copy in zip(send_back, send_on):
            arrived.wait_recv()
            copy.start()

    line_finish(0)
    line_start(1)

    @pl.when(has_prev)
    def _():
        send_inv.wait_recv()

    def left_product(cols):
        left[:, cols] = mm(even[...], inv_in[:, cols]).astype(BF16)

    column_blocks(left_product)
    line_finish(1)
    line_start(2)

    @pl.when(has_prev)
    def _():
        send_up.wait_recv()
        send_places.wait_recv()

    load_slots_in = load(places_in, slots_in, 8)
    load_slots_in.wait()
    expand(wide, lambda s: up_in[s], slots_in, 0)

    def diag_product(cols):
        new_diag[:, cols] = (rest[:, cols] - mm(left[...], wide[:, cols])).astype(BF16)

    column_blocks(diag_product)

    @pl.when(third)
    def _():
        for arrived, copy in zip(send_back, send_home):
            arrived.wait_recv()
            copy.start()

    line_finish(2)

    @pl.when(has_prev)
    def _():
        send_down[0].wait_recv()

    expand(down_wide, lambda s: first_in[s], slots_in, 1, HALF)

    @pl.when(far_end | second | third)
    def _():
        for copy in send_back:
            copy.wait_send()

    @pl.when(has_next & ~far_end)
    def _():
        for copy in send_down:
            copy.wait_send()

    @pl.when(has_next)
    def _():
        send_inv.wait_send()
        send_up.wait_send()
        send_places.wait_send()

    @pl.when(has_prev)
    def _():
        send_down[1].wait_recv()


def exchange(sizes, *operands):
    dense = pltpu.VMEM((P_SIZE, P_SIZE), BF16)
    tiles = pltpu.VMEM((KT, TILE, TILE), BF16)
    half = pltpu.VMEM((HALF, TILE, TILE), BF16)
    row = pltpu.VMEM((1, P_SIZE), F32)
    rows = pltpu.VMEM((len(STEPS), 1, P_SIZE), F32)
    columns = sizes[0] * sizes[1] // (2 * DEPTH)
    return pl.pallas_call(
        functools.partial(exchange_kernel, sizes),
        name="exchange",
        out_shape=(
            dense,
            dense,
            half,
            pltpu.VMEM((NT, TILE), I32),
            dense,
            dense,
            row,
        ),
        in_specs=[pl.BlockSpec(memory_space=pltpu.HBM)] * 7,
        out_specs=(pl.BlockSpec(memory_space=pltpu.VMEM),) * 7,
        scratch_shapes=[
            pltpu.VMEM((2, KT), I32),
            pltpu.VMEM((2, KT), I32),
            pltpu.VMEM((1, KT), I32),
            pltpu.VMEM((2, KT, TILE, TILE), BF16),
            pltpu.VMEM((2, KT, TILE, TILE), BF16),
            tiles,
            dense,
            pltpu.VMEM((NT, TILE), I32),
            pltpu.SMEM((NT, TILE), I32),
            pltpu.SMEM((NT, TILE), I32),
            dense,
            tiles,
            half,
            tiles,
            dense,
            dense,
            dense,
            pltpu.VMEM((P_SIZE, P_SIZE), F32),
            row,
            row,
            row,
            pltpu.VMEM((columns - 1, 1, P_SIZE), F32),
            rows,
            rows,
            rows,
            rows,
            pltpu.SemaphoreType.DMA((9,)),
            pltpu.SemaphoreType.DMA((COLUMN + columns - 1,)),
            pltpu.SemaphoreType.DMA((COLUMN + columns - 1,)),
            pltpu.SemaphoreType.REGULAR,
            pltpu.SemaphoreType.REGULAR,
        ],
        compiler_params=pltpu.CompilerParams(
            collective_id=0, has_side_effects=True, vmem_limit_bytes=44 << 20
        ),
    )(*(pltpu.with_memory_space_constraint(x, pltpu.HBM) for x in operands))


def finish_kernel(
    places,
    left,
    wide_in,
    tiles,
    up_in,
    diag_in,
    sums_in,
    new_diag,
    new_up,
    new_down,
    sums,
    wide,
    out,
    sem,
):
    copies = [
        pltpu.make_async_copy(up_in, new_up.at[0], sem.at[0]),
        pltpu.make_async_copy(diag_in, new_diag.at[0], sem.at[1]),
    ]
    for copy in copies:
        copy.start()
    sums[...] = sums_in[...]
    for k in range(HALF, KT):
        p = jnp.clip(places[5, k], 0, NT * NT - 1)
        r = pl.multiple_of((p >> 3) * TILE, TILE)
        c = pl.multiple_of((p & 7) * TILE, TILE)
        wide[pl.ds(r, TILE), pl.ds(c, TILE)] = tiles[k - HALF]
    for b in range(P_SIZE // WIDE):
        rows = pl.ds(b * WIDE, WIDE)
        out[rows] = (-mm(left[rows], wide[...])).astype(BF16)
        copy = pltpu.make_async_copy(out.at[rows], new_down.at[0, rows], sem.at[2 + b])
        copy.start()
        copies.append(copy)
    for copy in copies:
        copy.wait()


def finish(places, left, wide, *operands):
    vmem = pl.BlockSpec(memory_space=pltpu.VMEM)
    hbm = pl.BlockSpec(memory_space=pltpu.HBM)
    square = jax.ShapeDtypeStruct((1, P_SIZE, P_SIZE), BF16)
    return pl.pallas_call(
        finish_kernel,
        name="finish",
        out_shape=(
            square,
            square,
            square,
            jax.ShapeDtypeStruct((1, P_SIZE), F32),
            pltpu.VMEM((P_SIZE, P_SIZE), BF16),
        ),
        in_specs=[pl.BlockSpec(memory_space=pltpu.SMEM)] + [vmem] * 6,
        out_specs=(hbm, hbm, hbm, vmem, vmem),
        scratch_shapes=[
            pltpu.VMEM((P_SIZE, P_SIZE), BF16),
            pltpu.SemaphoreType.DMA((2 + P_SIZE // WIDE,)),
        ],
        input_output_aliases={2: 4},
        compiler_params=pltpu.CompilerParams(vmem_limit_bytes=16 << 20),
    )(places, left, wide, *operands)


def local(sizes, up_tiles, up_at, down_tiles, down_at, diag_tiles, diag_at, odd_inverse):
    left, wide, down_in, places_in, new_up, new_diag, sums = exchange(
        sizes, up_at, down_at, diag_at, up_tiles, down_tiles, diag_tiles, odd_inverse
    )
    return finish(places_in, left, wide, down_in, new_up, new_diag, sums)[:4]


def solution(mesh):
    sizes = (mesh.shape["grp"], mesh.shape["lev"])
    return jax.shard_map(
        functools.partial(local, sizes),
        mesh=mesh,
        in_specs=(
            P(AXES, None, None, None),
            P(AXES, None),
            P(AXES, None, None, None),
            P(AXES, None),
            P(AXES, None, None, None),
            P(AXES, None),
            P(AXES, None, None),
        ),
        out_specs=(
            P(AXES, None, None),
            P(AXES, None, None),
            P(AXES, None, None),
            P(AXES, None),
        ),
        check_vma=False,
    )
```

```python
import functools

import jax
import jax.numpy as jnp
from jax import lax
from jax.experimental import pallas as pl
from jax.experimental.pallas import tpu as pltpu
from jax.sharding import PartitionSpec as P

TILE = 128
NT = 8
P_SIZE = 1024
KT = 24
HALF = KT // 2
WIDE = 256
DEPTH = 8
SIDE = 4
STEPS = (1, 2, 4)
AXES = ("grp", "lev")
MESH = pl.DeviceIdType.MESH
F32 = jnp.float32
BF16 = jnp.bfloat16
I32 = jnp.int32
INV, UP, PLACE, DOWN, HOP, PAIR, RESULT, FIRST, LINE, COLUMN = 0, 2, 3, 4, 6, 7, 8, 9, 10, 16


def mm(a, b):
    return jnp.dot(a, b, preferred_element_type=F32)


def column_blocks(body, wide=WIDE):
    def step(b, carry):
        body(pl.ds(pl.multiple_of(b * wide, wide), wide))
        return carry

    lax.fori_loop(0, P_SIZE // wide, step, 0)


def expand(dense, tile_of, slots, row, below=KT, unroll=1):
    def tile_row(r, carry):
        rows = pl.ds(pl.multiple_of(r * TILE, TILE), TILE)
        for c in range(NT):
            slot = slots[row, r * NT + c]
            tile = tile_of(jnp.clip(slot, 0, below - 1))
            here = (slot >= 0) & (slot < below)
            dense[rows, c * TILE : (c + 1) * TILE] = jnp.where(here, tile, jnp.zeros_like(tile))
        return carry

    lax.fori_loop(0, NT, tile_row, 0, unroll=unroll)


def slot_row(places):
    number = lax.broadcasted_iota(I32, (KT, KT), 0)
    lane = lax.broadcasted_iota(I32, (KT, KT), 1)
    spread = jnp.broadcast_to(places, (KT, KT))
    column = jnp.sum(jnp.where(number == lane, spread, 0), axis=1, keepdims=True)
    position = lax.broadcasted_iota(I32, (KT, TILE), 1)
    index = lax.broadcasted_iota(I32, (KT, TILE), 0) + 1
    hit = jnp.broadcast_to(column, (KT, TILE)) == position
    return jnp.max(jnp.where(hit, index, 0), axis=0, keepdims=True) - 1


def exchange_kernel(
    sizes,
    up_at,
    down_at,
    diag_at,
    up,
    down,
    diag,
    inv,
    left,
    down_wide,
    down_in,
    places_in,
    new_up,
    new_diag,
    sums,
    up_at_v,
    down_at_v,
    diag_at_v,
    up_v,
    down_v,
    diag_v,
    inv_v,
    places,
    slots,
    slots_in,
    inv_in,
    up_in,
    first_in,
    hop,
    wide,
    even,
    prod,
    rest,
    term,
    pair,
    pair_in,
    before,
    upto,
    shared,
    first_total,
    columns_in,
    rising,
    falling,
    rising_in,
    falling_in,
    local_sem,
    send_sem,
    recv_sem,
    near_sem,
    far_sem,
):
    groups, inner = sizes
    count = groups * inner
    lev = lax.axis_index("lev")
    grp = lax.axis_index("grp")
    me = grp * inner + lev
    core = lev % 2
    z = (lev // 2) % DEPTH
    column = me // (2 * DEPTH)
    columns = count // (2 * DEPTH)

    def place_of(index):
        return (index // inner, index % inner)

    def up_line(distance):
        return place_of(me + 2 * distance)

    other_core = place_of(me + 1 - 2 * core)
    same_z = [
        place_of(((column + j) % columns) * 2 * DEPTH + 2 * z + core) for j in range(1, columns)
    ]
    has_next, has_prev = me < count - 1, me > 0
    inside = column < columns - 1
    first_core = core == 0
    meets = first_core & (z >= 1)
    giver = (core == 1) & (z == 7) & inside
    far_end = first_core & (z == 7) & inside
    second = first_core & (z == 4) & inside
    third = first_core & (z == 1) & inside
    hop_from = first_core & (z == 0) & has_prev
    target = place_of((column + 1) * 2 * DEPTH)
    holder = place_of((column - 1) * 2 * DEPTH + 2)

    def load(source, target, sem):
        copy = pltpu.make_async_copy(source, target, local_sem.at[sem])
        copy.start()
        return copy

    barrier = pltpu.get_barrier_semaphore()

    def tell(device):
        pl.semaphore_signal(barrier, inc=1, device_id=device, device_id_type=MESH)

    def tell_if(condition, device):
        @pl.when(condition)
        def _():
            tell(device)

    tell_if(has_prev, place_of(me - 1))
    tell(other_core)
    tell_if(first_core & (z >= 1), up_line(-1))
    for step in STEPS:
        tell_if(first_core & (z + step < DEPTH), up_line(step))
    tell_if(second | third, up_line(3))
    tell_if(hop_from, holder)

    tell_if(first_core & (z == 1), up_line(-1))

    @pl.when(meets)
    def _():
        for device in same_z:
            tell(device)

    load_up_at = load(up_at, up_at_v, 0)
    load_down_at = load(down_at, down_at_v, 1)
    load_diag_at = load(diag_at, diag_at_v, 2)
    load_up = load(up, up_v, 3)
    load_inv = load(inv.at[0], inv_v, 4)
    load_down = load(down, down_v, 5)
    load_diag = load(diag.at[0], diag_v, 6)

    expected = 1 + has_next.astype(I32) + (far_end | second | third).astype(I32)
    line = len(same_z) * (z >= 1).astype(I32)
    for condition in (z == 0, z < DEPTH - 1, z >= 1, z >= 2, z >= 4):
        line += condition.astype(I32)
    expected += (1 - core) * line
    pl.semaphore_wait(barrier, expected)

    def remote(source, target, send, recv, device):
        return pltpu.make_async_remote_copy(
            src_ref=source,
            dst_ref=target,
            send_sem=send_sem.at[send],
            recv_sem=recv_sem.at[recv],
            device_id=device,
            device_id_type=MESH,
        )

    following = place_of(me + 1)
    halves = [pl.ds(c * HALF, HALF) for c in range(2)]
    tall = [pl.ds(c * (P_SIZE // 2), P_SIZE // 2) for c in range(2)]
    send_inv = [
        remote(inv.at[0, rows], inv_in.at[rows], INV + c, INV + c, following)
        for c, rows in enumerate(tall)
    ]
    send_up = remote(up.at[1], up_in, UP, UP, following)
    send_places = remote(places, places_in, PLACE, PLACE, following)
    send_down = [
        remote(down.at[1, h], landing, DOWN + c, DOWN + c, following)
        for c, (h, landing) in enumerate(zip(halves, (first_in, down_in)))
    ]
    send_across = remote(down.at[1, halves[0]], hop, HOP, HOP, other_core)
    send_back = remote(hop, hop, HOP, HOP, up_line(-3))
    send_home = remote(hop, first_in, HOP, DOWN, target)

    def forward(condition, copy):
        @pl.when(condition)
        def _():
            send_across.wait_recv()
            copy.start()

    @pl.when(giver)
    def _():
        send_across.start()

    @pl.when(has_next)
    def _():
        send_inv[0].start()

    load_up_at.wait()
    load_down_at.wait()
    load_diag_at.wait()
    places[...] = jnp.full_like(places, -1)
    places[0:1] = slot_row(up_at_v[1:2])
    places[1:2] = slot_row(down_at_v[1:2])
    places[2:3] = slot_row(up_at_v[0:1])
    places[3:4] = slot_row(down_at_v[0:1])
    places[4:5] = slot_row(diag_at_v[...])
    places[5:6, 0:KT] = down_at_v[1:2]

    @pl.when(first_core & (z >= 1))
    def _():
        pl.semaphore_signal(near_sem, inc=1, device_id=up_line(-1), device_id_type=MESH)

    @pl.when(me == 0)
    def _():
        inv_in[...] = jnp.zeros_like(inv_in)
        up_in[...] = jnp.zeros_like(up_in)
        first_in[...] = jnp.zeros_like(first_in)
        down_in[...] = jnp.zeros_like(down_in)
        places_in[...] = jnp.zeros_like(places_in)

    load_slots = load(places, slots, 7)
    load_slots.wait()
    load_up.wait()
    expand(wide, lambda s: up_v[1, s], slots, 0)
    load_inv.wait()

    def odd_product(cols):
        prod[:, cols] = mm(inv_v[...], wide[:, cols]).astype(BF16)

    column_blocks(odd_product)

    forward(far_end, send_back)

    @pl.when(first_core & (z < DEPTH - 1))
    def _():
        pl.semaphore_wait(near_sem, 1)

    @pl.when(first_core & (z >= 2))
    def _():
        pl.semaphore_signal(far_sem, inc=1, device_id=up_line(-2), device_id_type=MESH)

    expand(even, lambda s: up_v[0, s], slots, 2)
    weight = (count + 2 * me).astype(F32) / count

    def up_product(cols):
        out = (-mm(even[...], prod[:, cols])).astype(BF16)
        new_up[:, cols] = out
        mean = jnp.sum(out.astype(F32), axis=0, keepdims=True) / P_SIZE
        term[:, cols] = weight * mean

    column_blocks(up_product)

    send_term = remote(term, pair_in, PAIR, PAIR, other_core)

    @pl.when(~first_core)
    def _():
        send_term.start()

    @pl.when(has_next)
    def _():
        send_inv[1].start()
        send_places.start()
        send_up.start()

    @pl.when(has_next & ~giver)
    def _():
        send_down[0].start()

    @pl.when(has_next)
    def _():
        send_down[1].start()

    load_down.wait()
    expand(wide, lambda s: down_v[1, s], slots, 1)
    send_pair = [
        remote(shared, columns_in.at[j], COLUMN + j, COLUMN + j, device)
        for j, device in enumerate(same_z)
    ]
    column_blocks(odd_product)

    @pl.when(first_core)
    def _():
        send_term.wait_recv()
        pair[...] = term[...] + pair_in[...]
        shared[...] = pair[...]

    send_first = remote(pair, first_total, FIRST, FIRST, up_line(1))

    @pl.when(first_core & (z == 0))
    def _():
        send_first.start()

    @pl.when(first_core & (z == 1))
    def _():
        send_first.wait_recv()
        shared[...] += first_total[...]

    @pl.when(meets)
    def _():
        for copy in send_pair:
            copy.start()

    @pl.when(first_core & (z < DEPTH - 2))
    def _():
        pl.semaphore_wait(far_sem, 1)

    load_diag.wait()
    expand(wide, lambda s: diag_v[s], slots, 4)

    def rest_product(cols):
        rest[:, cols] = wide[:, cols].astype(F32) - mm(even[...], prod[:, cols])

    column_blocks(rest_product)
    forward(second, send_back)

    before[...] = jnp.zeros_like(before)

    @pl.when(meets)
    def _():
        for copy in send_pair:
            copy.wait()
        for j in range(columns - 1):
            got = columns_in[j]
            before[...] += jnp.where(column > j, got, jnp.zeros_like(got))

    @pl.when(first_core & (z == 0))
    def _():
        send_first.wait_send()

    @pl.when(first_core)
    def _():
        rising[0] = before[...] + pair[...]
        falling[0] = before[...]

    def line_copies(n):
        up_step = remote(
            rising.at[n], rising_in.at[n], LINE + 2 * n, LINE + 2 * n, up_line(STEPS[n])
        )
        down_step = remote(
            falling.at[n],
            falling_in.at[n],
            LINE + 2 * n + 1,
            LINE + 2 * n + 1,
            up_line(-STEPS[n]),
        )
        return up_step, down_step

    def line_start(n):
        up_step, down_step = line_copies(n)

        @pl.when(first_core & (z + STEPS[n] < DEPTH))
        def _():
            up_step.start()

        @pl.when(first_core & (z >= STEPS[n]))
        def _():
            down_step.start()

    def line_finish(n):
        up_step, down_step = line_copies(n)
        last = n == len(STEPS) - 1
        if not last:
            rising[n + 1] = rising[n]
            falling[n + 1] = falling[n]

        @pl.when(first_core & (z >= STEPS[n]))
        def _():
            down_step.wait_send()
            up_step.wait_recv()
            before[...] += rising_in[n]
            if not last:
                rising[n + 1] += rising_in[n]

        @pl.when(first_core & (z + STEPS[n] < DEPTH))
        def _():
            up_step.wait_send()
            down_step.wait_recv()
            before[...] += falling_in[n]
            if not last:
                falling[n + 1] += falling_in[n]

    line_start(0)
    expand(even, lambda s: down_v[0, s], slots, 3)

    line_finish(0)
    line_start(1)

    @pl.when(has_prev)
    def _():
        for copy in send_inv:
            copy.wait_recv()

    def left_product(cols):
        left[:, cols] = mm(even[...], inv_in[:, cols]).astype(BF16)

    column_blocks(left_product, 2 * WIDE)
    line_finish(1)
    line_start(2)
    forward(third, send_home)
    line_finish(2)
    send_result = remote(upto, pair_in, RESULT, RESULT, other_core)

    @pl.when(first_core)
    def _():
        upto[...] = before[...] + term[...]
        sums[...] = upto[...]
        send_result.start()


    def lay_first_half():
        send_down[0].wait_recv()
        expand(down_wide, lambda s: first_in[s], slots_in, 1, HALF, unroll=True)

    @pl.when(has_prev)
    def _():
        send_places.wait_recv()

    load_slots_in = load(places_in, slots_in, 8)
    load_slots_in.wait()
    pl.when(hop_from)(lay_first_half)

    @pl.when(has_prev)
    def _():
        send_up.wait_recv()

    expand(wide, lambda s: up_in[s], slots_in, 0, unroll=True)

    def diag_product(cols):
        new_diag[:, cols] = (rest[:, cols] - mm(left[...], wide[:, cols])).astype(BF16)

    column_blocks(diag_product, 2 * WIDE)

    pl.when(has_prev & ~hop_from)(lay_first_half)

    @pl.when(me == 0)
    def _():
        down_wide[...] = jnp.zeros_like(down_wide)

    @pl.when(giver | far_end | second | third)
    def _():
        send_back.wait_send()

    @pl.when(has_next & ~giver)
    def _():
        send_down[0].wait_send()

    @pl.when(has_next)
    def _():
        for copy in send_inv:
            copy.wait_send()
        send_up.wait_send()
        send_places.wait_send()
        send_down[1].wait_send()

    @pl.when(first_core)
    def _():
        send_result.wait_send()

    @pl.when(~first_core)
    def _():
        send_term.wait_send()
        send_result.wait_recv()
        sums[...] = term[...] + pair_in[...]

    @pl.when(has_prev)
    def _():
        send_down[1].wait_recv()


def exchange(sizes, *operands):
    dense = pltpu.VMEM((P_SIZE, P_SIZE), BF16)
    tiles = pltpu.VMEM((KT, TILE, TILE), BF16)
    half = pltpu.VMEM((HALF, TILE, TILE), BF16)
    row = pltpu.VMEM((1, P_SIZE), F32)
    rows = pltpu.VMEM((len(STEPS), 1, P_SIZE), F32)
    columns = sizes[0] * sizes[1] // (2 * DEPTH)
    return pl.pallas_call(
        functools.partial(exchange_kernel, sizes),
        name="exchange",
        out_shape=(
            dense,
            dense,
            half,
            pltpu.VMEM((NT, TILE), I32),
            dense,
            dense,
            row,
        ),
        in_specs=[pl.BlockSpec(memory_space=pltpu.HBM)] * 7,
        out_specs=(pl.BlockSpec(memory_space=pltpu.VMEM),) * 7,
        scratch_shapes=[
            pltpu.VMEM((2, KT), I32),
            pltpu.VMEM((2, KT), I32),
            pltpu.VMEM((1, KT), I32),
            pltpu.VMEM((2, KT, TILE, TILE), BF16),
            pltpu.VMEM((2, KT, TILE, TILE), BF16),
            tiles,
            dense,
            pltpu.VMEM((NT, TILE), I32),
            pltpu.SMEM((NT, TILE), I32),
            pltpu.SMEM((NT, TILE), I32),
            dense,
            tiles,
            half,
            half,
            dense,
            dense,
            dense,
            pltpu.VMEM((P_SIZE, P_SIZE), F32),
            row,
            row,
            row,
            row,
            row,
            row,
            row,
            pltpu.VMEM((columns - 1, 1, P_SIZE), F32),
            rows,
            rows,
            rows,
            rows,
            pltpu.SemaphoreType.DMA((9,)),
            pltpu.SemaphoreType.DMA((COLUMN + columns - 1,)),
            pltpu.SemaphoreType.DMA((COLUMN + columns - 1,)),
            pltpu.SemaphoreType.REGULAR,
            pltpu.SemaphoreType.REGULAR,
        ],
        compiler_params=pltpu.CompilerParams(
            collective_id=0, has_side_effects=True, vmem_limit_bytes=44 << 20
        ),
    )(*(pltpu.with_memory_space_constraint(x, pltpu.HBM) for x in operands))


def finish_kernel(
    places,
    left,
    wide_in,
    tiles,
    up_in,
    diag_in,
    sums_in,
    new_diag,
    new_up,
    new_down,
    sums,
    wide,
    out,
    sem,
):
    copies = [
        pltpu.make_async_copy(up_in, new_up.at[0], sem.at[0]),
        pltpu.make_async_copy(diag_in, new_diag.at[0], sem.at[1]),
    ]
    for copy in copies:
        copy.start()
    sums[...] = sums_in[...]
    for k in range(HALF, KT):
        p = jnp.clip(places[5, k], 0, NT * NT - 1)
        r = pl.multiple_of((p >> 3) * TILE, TILE)
        c = pl.multiple_of((p & 7) * TILE, TILE)
        wide[pl.ds(r, TILE), pl.ds(c, TILE)] = tiles[k - HALF]
    for b in range(P_SIZE // WIDE):
        rows = pl.ds(b * WIDE, WIDE)
        out[rows] = (-mm(left[rows], wide[...])).astype(BF16)
        copy = pltpu.make_async_copy(out.at[rows], new_down.at[0, rows], sem.at[2 + b])
        copy.start()
        copies.append(copy)
    for copy in copies:
        copy.wait()


def finish(places, left, wide, *operands):
    vmem = pl.BlockSpec(memory_space=pltpu.VMEM)
    hbm = pl.BlockSpec(memory_space=pltpu.HBM)
    square = jax.ShapeDtypeStruct((1, P_SIZE, P_SIZE), BF16)
    return pl.pallas_call(
        finish_kernel,
        name="finish",
        out_shape=(
            square,
            square,
            square,
            jax.ShapeDtypeStruct((1, P_SIZE), F32),
            pltpu.VMEM((P_SIZE, P_SIZE), BF16),
        ),
        in_specs=[pl.BlockSpec(memory_space=pltpu.SMEM)] + [vmem] * 6,
        out_specs=(hbm, hbm, hbm, vmem, vmem),
        scratch_shapes=[
            pltpu.VMEM((P_SIZE, P_SIZE), BF16),
            pltpu.SemaphoreType.DMA((2 + P_SIZE // WIDE,)),
        ],
        input_output_aliases={2: 4},
        compiler_params=pltpu.CompilerParams(vmem_limit_bytes=16 << 20),
    )(places, left, wide, *operands)


def local(sizes, up_tiles, up_at, down_tiles, down_at, diag_tiles, diag_at, odd_inverse):
    left, wide, down_in, places_in, new_up, new_diag, sums = exchange(
        sizes, up_at, down_at, diag_at, up_tiles, down_tiles, diag_tiles, odd_inverse
    )
    return finish(places_in, left, wide, down_in, new_up, new_diag, sums)[:4]


def solution(mesh):
    sizes = (mesh.shape["grp"], mesh.shape["lev"])
    return jax.shard_map(
        functools.partial(local, sizes),
        mesh=mesh,
        in_specs=(
            P(AXES, None, None, None),
            P(AXES, None),
            P(AXES, None, None, None),
            P(AXES, None),
            P(AXES, None, None, None),
            P(AXES, None),
            P(AXES, None, None),
        ),
        out_specs=(
            P(AXES, None, None),
            P(AXES, None, None),
            P(AXES, None, None),
            P(AXES, None),
        ),
        check_vma=False,
    )
```

```python
import functools

import jax
import jax.numpy as jnp
from jax import lax
from jax.experimental import pallas as pl
from jax.experimental.pallas import tpu as pltpu
from jax.sharding import PartitionSpec as P

TILE = 128
NT = 8
P_SIZE = 1024
KT = 24
HALF = KT // 2
WIDE = 256
DEPTH = 8
SIDE = 4
STEPS = (1, 2, 4)
AXES = ("grp", "lev")
MESH = pl.DeviceIdType.MESH
F32 = jnp.float32
BF16 = jnp.bfloat16
I32 = jnp.int32
INV, UP, PLACE, DOWN, HOP, PAIR, RESULT, FIRST, LINE, COLUMN = 0, 2, 3, 4, 6, 7, 8, 9, 10, 16


def mm(a, b):
    return jnp.dot(a, b, preferred_element_type=F32)


def column_blocks(body, wide=WIDE):
    def step(b, carry):
        body(pl.ds(pl.multiple_of(b * wide, wide), wide))
        return carry

    lax.fori_loop(0, P_SIZE // wide, step, 0)


def expand(dense, tile_of, slots, row, below=KT, unroll=1):
    def tile_row(r, carry):
        rows = pl.ds(pl.multiple_of(r * TILE, TILE), TILE)
        for c in range(NT):
            slot = slots[row, r * NT + c]
            tile = tile_of(jnp.clip(slot, 0, below - 1))
            here = (slot >= 0) & (slot < below)
            dense[rows, c * TILE : (c + 1) * TILE] = jnp.where(here, tile, jnp.zeros_like(tile))
        return carry

    lax.fori_loop(0, NT, tile_row, 0, unroll=unroll)


def slot_row(places):
    number = lax.broadcasted_iota(I32, (KT, KT), 0)
    lane = lax.broadcasted_iota(I32, (KT, KT), 1)
    spread = jnp.broadcast_to(places, (KT, KT))
    column = jnp.sum(jnp.where(number == lane, spread, 0), axis=1, keepdims=True)
    position = lax.broadcasted_iota(I32, (KT, TILE), 1)
    index = lax.broadcasted_iota(I32, (KT, TILE), 0) + 1
    hit = jnp.broadcast_to(column, (KT, TILE)) == position
    return jnp.max(jnp.where(hit, index, 0), axis=0, keepdims=True) - 1


def exchange_kernel(
    sizes,
    up_at,
    down_at,
    diag_at,
    up,
    down,
    diag,
    inv,
    left,
    down_wide,
    down_in,
    places_in,
    new_up,
    new_diag,
    sums,
    up_at_v,
    down_at_v,
    diag_at_v,
    up_v,
    down_v,
    diag_v,
    inv_v,
    places,
    slots,
    slots_in,
    inv_in,
    up_in,
    first_in,
    hop,
    wide,
    even,
    prod,
    rest,
    term,
    pair,
    pair_in,
    before,
    upto,
    shared,
    first_total,
    columns_in,
    rising,
    falling,
    rising_in,
    falling_in,
    local_sem,
    send_sem,
    recv_sem,
    near_sem,
    far_sem,
):
    groups, inner = sizes
    count = groups * inner
    lev = lax.axis_index("lev")
    grp = lax.axis_index("grp")
    me = grp * inner + lev
    core = lev % 2
    z = (lev // 2) % DEPTH
    column = me // (2 * DEPTH)
    columns = count // (2 * DEPTH)

    def place_of(index):
        return (index // inner, index % inner)

    def up_line(distance):
        return place_of(me + 2 * distance)

    other_core = place_of(me + 1 - 2 * core)
    same_z = [
        place_of(((column + j) % columns) * 2 * DEPTH + 2 * z + core) for j in range(1, columns)
    ]
    has_next, has_prev = me < count - 1, me > 0
    inside = column < columns - 1
    first_core = core == 0
    meets = first_core & (z >= 1)
    giver = (core == 1) & (z == 7) & inside
    far_end = first_core & (z == 7) & inside
    second = first_core & (z == 4) & (column >= 1)
    third = first_core & (z == 1) & (column >= 1)
    hop_from = first_core & (z == 0) & has_prev
    middle = place_of((column + 1) * 2 * DEPTH + 8)
    giving = place_of((column - 1) * 2 * DEPTH + 14)

    def load(source, target, sem):
        copy = pltpu.make_async_copy(source, target, local_sem.at[sem])
        copy.start()
        return copy

    barrier = pltpu.get_barrier_semaphore()

    def tell(device):
        pl.semaphore_signal(barrier, inc=1, device_id=device, device_id_type=MESH)

    def tell_if(condition, device):
        @pl.when(condition)
        def _():
            tell(device)

    tell_if(has_prev, place_of(me - 1))
    tell(other_core)
    tell_if(first_core & (z >= 1), up_line(-1))
    for step in STEPS:
        tell_if(first_core & (z + step < DEPTH), up_line(step))
    tell_if(third, up_line(3))
    tell_if(second, giving)

    tell_if(first_core & (z == 1), up_line(-1))

    @pl.when(meets)
    def _():
        for device in same_z:
            tell(device)

    load_up_at = load(up_at, up_at_v, 0)
    load_down_at = load(down_at, down_at_v, 1)
    load_diag_at = load(diag_at, diag_at_v, 2)
    load_up = load(up, up_v, 3)
    load_inv = load(inv.at[0], inv_v, 4)
    load_down = load(down, down_v, 5)
    load_diag = load(diag.at[0], diag_v, 6)

    expected = 1 + has_next.astype(I32) + (far_end | second).astype(I32)
    line = len(same_z) * (z >= 1).astype(I32)
    for condition in (z == 0, z < DEPTH - 1, z >= 1, z >= 2, z >= 4):
        line += condition.astype(I32)
    expected += (1 - core) * line
    pl.semaphore_wait(barrier, expected)

    def remote(source, target, send, recv, device):
        return pltpu.make_async_remote_copy(
            src_ref=source,
            dst_ref=target,
            send_sem=send_sem.at[send],
            recv_sem=recv_sem.at[recv],
            device_id=device,
            device_id_type=MESH,
        )

    following = place_of(me + 1)
    halves = [pl.ds(c * HALF, HALF) for c in range(2)]
    tall = [pl.ds(c * (P_SIZE // 2), P_SIZE // 2) for c in range(2)]
    send_inv = [
        remote(inv.at[0, rows], inv_in.at[rows], INV + c, INV + c, following)
        for c, rows in enumerate(tall)
    ]
    send_up = remote(up.at[1], up_in, UP, UP, following)
    send_places = remote(places, places_in, PLACE, PLACE, following)
    send_down = [
        remote(down.at[1, h], landing, DOWN + c, DOWN + c, following)
        for c, (h, landing) in enumerate(zip(halves, (first_in, down_in)))
    ]
    send_across = remote(down.at[1, halves[0]], hop, HOP, HOP, other_core)
    send_over = remote(hop, hop, HOP, HOP, middle)
    send_back = remote(hop, hop, HOP, HOP, up_line(-3))
    send_home = remote(hop, first_in, HOP, DOWN, up_line(-1))

    def forward(condition, copy):
        @pl.when(condition)
        def _():
            send_across.wait_recv()
            copy.start()

    @pl.when(giver)
    def _():
        send_across.start()

    @pl.when(has_next)
    def _():
        send_inv[0].start()

    load_up_at.wait()
    load_down_at.wait()
    load_diag_at.wait()
    places[...] = jnp.full_like(places, -1)
    places[0:1] = slot_row(up_at_v[1:2])
    places[1:2] = slot_row(down_at_v[1:2])
    places[2:3] = slot_row(up_at_v[0:1])
    places[3:4] = slot_row(down_at_v[0:1])
    places[4:5] = slot_row(diag_at_v[...])
    places[5:6, 0:KT] = down_at_v[1:2]

    @pl.when(first_core & (z >= 1))
    def _():
        pl.semaphore_signal(near_sem, inc=1, device_id=up_line(-1), device_id_type=MESH)

    @pl.when(me == 0)
    def _():
        inv_in[...] = jnp.zeros_like(inv_in)
        up_in[...] = jnp.zeros_like(up_in)
        first_in[...] = jnp.zeros_like(first_in)
        down_in[...] = jnp.zeros_like(down_in)
        places_in[...] = jnp.zeros_like(places_in)

    load_slots = load(places, slots, 7)
    load_slots.wait()
    load_up.wait()
    expand(wide, lambda s: up_v[1, s], slots, 0)
    forward(far_end, send_over)
    load_inv.wait()

    def odd_product(cols):
        prod[:, cols] = mm(inv_v[...], wide[:, cols]).astype(BF16)

    column_blocks(odd_product)

    @pl.when(first_core & (z < DEPTH - 1))
    def _():
        pl.semaphore_wait(near_sem, 1)

    @pl.when(first_core & (z >= 2))
    def _():
        pl.semaphore_signal(far_sem, inc=1, device_id=up_line(-2), device_id_type=MESH)

    expand(even, lambda s: up_v[0, s], slots, 2)
    weight = (count + 2 * me).astype(F32) / count

    def up_product(cols):
        out = (-mm(even[...], prod[:, cols])).astype(BF16)
        new_up[:, cols] = out
        mean = jnp.sum(out.astype(F32), axis=0, keepdims=True) / P_SIZE
        term[:, cols] = weight * mean

    column_blocks(up_product)

    send_term = remote(term, pair_in, PAIR, PAIR, other_core)

    @pl.when(~first_core)
    def _():
        send_term.start()

    @pl.when(has_next)
    def _():
        send_inv[1].start()
        send_places.start()
        send_up.start()

    @pl.when(has_next & ~giver)
    def _():
        send_down[0].start()

    @pl.when(has_next)
    def _():
        send_down[1].start()

    load_down.wait()
    expand(wide, lambda s: down_v[1, s], slots, 1)
    send_pair = [
        remote(shared, columns_in.at[j], COLUMN + j, COLUMN + j, device)
        for j, device in enumerate(same_z)
    ]
    column_blocks(odd_product)

    @pl.when(first_core)
    def _():
        send_term.wait_recv()
        pair[...] = term[...] + pair_in[...]
        shared[...] = pair[...]

    send_first = remote(pair, first_total, FIRST, FIRST, up_line(1))

    @pl.when(first_core & (z == 0))
    def _():
        send_first.start()

    @pl.when(first_core & (z == 1))
    def _():
        send_first.wait_recv()
        shared[...] += first_total[...]

    @pl.when(meets)
    def _():
        for copy in send_pair:
            copy.start()

    @pl.when(first_core & (z < DEPTH - 2))
    def _():
        pl.semaphore_wait(far_sem, 1)

    load_diag.wait()
    expand(wide, lambda s: diag_v[s], slots, 4)

    def rest_product(cols):
        rest[:, cols] = wide[:, cols].astype(F32) - mm(even[...], prod[:, cols])

    column_blocks(rest_product)
    forward(second, send_back)

    before[...] = jnp.zeros_like(before)

    @pl.when(meets)
    def _():
        for copy in send_pair:
            copy.wait()
        for j in range(columns - 1):
            got = columns_in[j]
            before[...] += jnp.where(column > j, got, jnp.zeros_like(got))

    @pl.when(first_core & (z == 0))
    def _():
        send_first.wait_send()

    @pl.when(first_core)
    def _():
        rising[0] = before[...] + pair[...]
        falling[0] = before[...]

    def line_copies(n):
        up_step = remote(
            rising.at[n], rising_in.at[n], LINE + 2 * n, LINE + 2 * n, up_line(STEPS[n])
        )
        down_step = remote(
            falling.at[n],
            falling_in.at[n],
            LINE + 2 * n + 1,
            LINE + 2 * n + 1,
            up_line(-STEPS[n]),
        )
        return up_step, down_step

    def line_start(n):
        up_step, down_step = line_copies(n)

        @pl.when(first_core & (z + STEPS[n] < DEPTH))
        def _():
            up_step.start()

        @pl.when(first_core & (z >= STEPS[n]))
        def _():
            down_step.start()

    def line_finish(n):
        up_step, down_step = line_copies(n)
        last = n == len(STEPS) - 1
        if not last:
            rising[n + 1] = rising[n]
            falling[n + 1] = falling[n]

        @pl.when(first_core & (z >= STEPS[n]))
        def _():
            down_step.wait_send()
            up_step.wait_recv()
            before[...] += rising_in[n]
            if not last:
                rising[n + 1] += rising_in[n]

        @pl.when(first_core & (z + STEPS[n] < DEPTH))
        def _():
            up_step.wait_send()
            down_step.wait_recv()
            before[...] += falling_in[n]
            if not last:
                falling[n + 1] += falling_in[n]

    line_start(0)
    expand(even, lambda s: down_v[0, s], slots, 3)

    line_finish(0)
    line_start(1)

    @pl.when(has_prev)
    def _():
        for copy in send_inv:
            copy.wait_recv()

    def left_product(cols):
        left[:, cols] = mm(even[...], inv_in[:, cols]).astype(BF16)

    column_blocks(left_product, 2 * WIDE)
    forward(third, send_home)
    line_finish(1)
    line_start(2)
    line_finish(2)
    send_result = remote(upto, pair_in, RESULT, RESULT, other_core)

    @pl.when(first_core)
    def _():
        upto[...] = before[...] + term[...]
        sums[...] = upto[...]
        send_result.start()


    def lay_first_half():
        send_down[0].wait_recv()
        expand(down_wide, lambda s: first_in[s], slots_in, 1, HALF, unroll=True)

    @pl.when(has_prev)
    def _():
        send_places.wait_recv()

    load_slots_in = load(places_in, slots_in, 8)
    load_slots_in.wait()
    pl.when(hop_from)(lay_first_half)

    @pl.when(has_prev)
    def _():
        send_up.wait_recv()

    expand(wide, lambda s: up_in[s], slots_in, 0, unroll=True)

    def diag_product(cols):
        new_diag[:, cols] = (rest[:, cols] - mm(left[...], wide[:, cols])).astype(BF16)

    column_blocks(diag_product, 2 * WIDE)

    pl.when(has_prev & ~hop_from)(lay_first_half)

    @pl.when(me == 0)
    def _():
        down_wide[...] = jnp.zeros_like(down_wide)

    @pl.when(giver | far_end | second | third)
    def _():
        send_back.wait_send()

    @pl.when(has_next & ~giver)
    def _():
        send_down[0].wait_send()

    @pl.when(has_next)
    def _():
        for copy in send_inv:
            copy.wait_send()
        send_up.wait_send()
        send_places.wait_send()
        send_down[1].wait_send()

    @pl.when(first_core)
    def _():
        send_result.wait_send()

    @pl.when(~first_core)
    def _():
        send_term.wait_send()
        send_result.wait_recv()
        sums[...] = term[...] + pair_in[...]

    @pl.when(has_prev)
    def _():
        send_down[1].wait_recv()


def exchange(sizes, *operands):
    dense = pltpu.VMEM((P_SIZE, P_SIZE), BF16)
    tiles = pltpu.VMEM((KT, TILE, TILE), BF16)
    half = pltpu.VMEM((HALF, TILE, TILE), BF16)
    row = pltpu.VMEM((1, P_SIZE), F32)
    rows = pltpu.VMEM((len(STEPS), 1, P_SIZE), F32)
    columns = sizes[0] * sizes[1] // (2 * DEPTH)
    return pl.pallas_call(
        functools.partial(exchange_kernel, sizes),
        name="exchange",
        out_shape=(
            dense,
            dense,
            half,
            pltpu.VMEM((NT, TILE), I32),
            dense,
            dense,
            row,
        ),
        in_specs=[pl.BlockSpec(memory_space=pltpu.HBM)] * 7,
        out_specs=(pl.BlockSpec(memory_space=pltpu.VMEM),) * 7,
        scratch_shapes=[
            pltpu.VMEM((2, KT), I32),
            pltpu.VMEM((2, KT), I32),
            pltpu.VMEM((1, KT), I32),
            pltpu.VMEM((2, KT, TILE, TILE), BF16),
            pltpu.VMEM((2, KT, TILE, TILE), BF16),
            tiles,
            dense,
            pltpu.VMEM((NT, TILE), I32),
            pltpu.SMEM((NT, TILE), I32),
            pltpu.SMEM((NT, TILE), I32),
            dense,
            tiles,
            half,
            half,
            dense,
            dense,
            dense,
            pltpu.VMEM((P_SIZE, P_SIZE), F32),
            row,
            row,
            row,
            row,
            row,
            row,
            row,
            pltpu.VMEM((columns - 1, 1, P_SIZE), F32),
            rows,
            rows,
            rows,
            rows,
            pltpu.SemaphoreType.DMA((9,)),
            pltpu.SemaphoreType.DMA((COLUMN + columns - 1,)),
            pltpu.SemaphoreType.DMA((COLUMN + columns - 1,)),
            pltpu.SemaphoreType.REGULAR,
            pltpu.SemaphoreType.REGULAR,
        ],
        compiler_params=pltpu.CompilerParams(
            collective_id=0, has_side_effects=True, vmem_limit_bytes=44 << 20
        ),
    )(*(pltpu.with_memory_space_constraint(x, pltpu.HBM) for x in operands))


def finish_kernel(
    places,
    left,
    wide_in,
    tiles,
    up_in,
    diag_in,
    sums_in,
    new_diag,
    new_up,
    new_down,
    sums,
    wide,
    out,
    sem,
):
    copies = [
        pltpu.make_async_copy(up_in, new_up.at[0], sem.at[0]),
        pltpu.make_async_copy(diag_in, new_diag.at[0], sem.at[1]),
    ]
    for copy in copies:
        copy.start()
    sums[...] = sums_in[...]
    for k in range(HALF, KT):
        p = jnp.clip(places[5, k], 0, NT * NT - 1)
        r = pl.multiple_of((p >> 3) * TILE, TILE)
        c = pl.multiple_of((p & 7) * TILE, TILE)
        wide[pl.ds(r, TILE), pl.ds(c, TILE)] = tiles[k - HALF]
    for b in range(P_SIZE // WIDE):
        rows = pl.ds(b * WIDE, WIDE)
        out[rows] = (-mm(left[rows], wide[...])).astype(BF16)
        copy = pltpu.make_async_copy(out.at[rows], new_down.at[0, rows], sem.at[2 + b])
        copy.start()
        copies.append(copy)
    for copy in copies:
        copy.wait()


def finish(places, left, wide, *operands):
    vmem = pl.BlockSpec(memory_space=pltpu.VMEM)
    hbm = pl.BlockSpec(memory_space=pltpu.HBM)
    square = jax.ShapeDtypeStruct((1, P_SIZE, P_SIZE), BF16)
    return pl.pallas_call(
        finish_kernel,
        name="finish",
        out_shape=(
            square,
            square,
            square,
            jax.ShapeDtypeStruct((1, P_SIZE), F32),
            pltpu.VMEM((P_SIZE, P_SIZE), BF16),
        ),
        in_specs=[pl.BlockSpec(memory_space=pltpu.SMEM)] + [vmem] * 6,
        out_specs=(hbm, hbm, hbm, vmem, vmem),
        scratch_shapes=[
            pltpu.VMEM((P_SIZE, P_SIZE), BF16),
            pltpu.SemaphoreType.DMA((2 + P_SIZE // WIDE,)),
        ],
        input_output_aliases={2: 4},
        compiler_params=pltpu.CompilerParams(vmem_limit_bytes=16 << 20),
    )(places, left, wide, *operands)


def local(sizes, up_tiles, up_at, down_tiles, down_at, diag_tiles, diag_at, odd_inverse):
    left, wide, down_in, places_in, new_up, new_diag, sums = exchange(
        sizes, up_at, down_at, diag_at, up_tiles, down_tiles, diag_tiles, odd_inverse
    )
    return finish(places_in, left, wide, down_in, new_up, new_diag, sums)[:4]


def solution(mesh):
    sizes = (mesh.shape["grp"], mesh.shape["lev"])
    return jax.shard_map(
        functools.partial(local, sizes),
        mesh=mesh,
        in_specs=(
            P(AXES, None, None, None),
            P(AXES, None),
            P(AXES, None, None, None),
            P(AXES, None),
            P(AXES, None, None, None),
            P(AXES, None),
            P(AXES, None, None),
        ),
        out_specs=(
            P(AXES, None, None),
            P(AXES, None, None),
            P(AXES, None, None),
            P(AXES, None),
        ),
        check_vma=False,
    )
```

```python
import functools

import jax
import jax.numpy as jnp
from jax import lax
from jax.experimental import pallas as pl
from jax.experimental.pallas import tpu as pltpu
from jax.sharding import PartitionSpec as P

TILE = 128
NT = 8
P_SIZE = 1024
KT = 24
FIRST_TILES = 14
WIDE = 256
DEPTH = 8
SIDE = 4
STEPS = (1, 2, 4)
AXES = ("grp", "lev")
MESH = pl.DeviceIdType.MESH
F32 = jnp.float32
BF16 = jnp.bfloat16
I32 = jnp.int32
INV, UP, PLACE, DOWN, HOP, HOME, PAIR, RESULT, FIRST, LINE, COLUMN = 0, 2, 3, 4, 6, 8, 10, 11, 12, 13, 19


def mm(a, b):
    return jnp.dot(a, b, preferred_element_type=F32)


def column_blocks(body, wide=WIDE):
    def step(b, carry):
        body(pl.ds(pl.multiple_of(b * wide, wide), wide))
        return carry

    lax.fori_loop(0, P_SIZE // wide, step, 0)


def expand(dense, tile_of, slots, row, below=KT, unroll=1):
    def tile_row(r, carry):
        rows = pl.ds(pl.multiple_of(r * TILE, TILE), TILE)
        for c in range(NT):
            slot = slots[row, r * NT + c]
            tile = tile_of(jnp.clip(slot, 0, below - 1))
            here = (slot >= 0) & (slot < below)
            dense[rows, c * TILE : (c + 1) * TILE] = jnp.where(here, tile, jnp.zeros_like(tile))
        return carry

    lax.fori_loop(0, NT, tile_row, 0, unroll=unroll)


def slot_row(places):
    number = lax.broadcasted_iota(I32, (KT, KT), 0)
    lane = lax.broadcasted_iota(I32, (KT, KT), 1)
    spread = jnp.broadcast_to(places, (KT, KT))
    column = jnp.sum(jnp.where(number == lane, spread, 0), axis=1, keepdims=True)
    position = lax.broadcasted_iota(I32, (KT, TILE), 1)
    index = lax.broadcasted_iota(I32, (KT, TILE), 0) + 1
    hit = jnp.broadcast_to(column, (KT, TILE)) == position
    return jnp.max(jnp.where(hit, index, 0), axis=0, keepdims=True) - 1


def exchange_kernel(
    sizes,
    up_at,
    down_at,
    diag_at,
    up,
    down,
    diag,
    inv,
    left,
    down_wide,
    down_in,
    slots_in,
    new_up,
    new_diag,
    sums,
    up_at_v,
    down_at_v,
    diag_at_v,
    up_v,
    down_v,
    diag_v,
    inv_v,
    places,
    slots,
    places_in,
    inv_in,
    up_in,
    first_in,
    hop,
    wide,
    even,
    prod,
    rest,
    term,
    pair,
    pair_in,
    before,
    upto,
    shared,
    first_total,
    columns_in,
    rising,
    falling,
    rising_in,
    falling_in,
    local_sem,
    send_sem,
    recv_sem,
    near_sem,
    far_sem,
):
    groups, inner = sizes
    count = groups * inner
    lev = lax.axis_index("lev")
    grp = lax.axis_index("grp")
    me = grp * inner + lev
    core = lev % 2
    z = (lev // 2) % DEPTH
    column = me // (2 * DEPTH)
    columns = count // (2 * DEPTH)

    def place_of(index):
        return (index // inner, index % inner)

    def up_line(distance):
        return place_of(me + 2 * distance)

    other_core = place_of(me + 1 - 2 * core)
    same_z = [
        place_of(((column + j) % columns) * 2 * DEPTH + 2 * z + core) for j in range(1, columns)
    ]
    has_next, has_prev = me < count - 1, me > 0
    inside = column < columns - 1
    first_core = core == 0
    meets = first_core & (z >= 1)
    giver = (core == 1) & (z == 7) & inside
    far_end = first_core & (z == 7) & inside
    second = first_core & (z == 4) & (column >= 1)
    third = first_core & (z == 1) & (column >= 1)
    hop_from = first_core & (z == 0) & has_prev
    middle = place_of((column + 1) * 2 * DEPTH + 8)
    giving = place_of((column - 1) * 2 * DEPTH + 14)

    def load(source, target, sem):
        copy = pltpu.make_async_copy(source, target, local_sem.at[sem])
        copy.start()
        return copy

    barrier = pltpu.get_barrier_semaphore()

    def tell(device):
        pl.semaphore_signal(barrier, inc=1, device_id=device, device_id_type=MESH)

    def tell_if(condition, device):
        @pl.when(condition)
        def _():
            tell(device)

    tell_if(has_prev, place_of(me - 1))
    tell(other_core)
    tell_if(first_core & (z >= 1), up_line(-1))
    for step in STEPS:
        tell_if(first_core & (z + step < DEPTH), up_line(step))
    tell_if(third, up_line(3))
    tell_if(second, giving)

    tell_if(first_core & (z == 1), up_line(-1))

    @pl.when(meets)
    def _():
        for device in same_z:
            tell(device)

    load_up_at = load(up_at, up_at_v, 0)
    load_down_at = load(down_at, down_at_v, 1)
    load_diag_at = load(diag_at, diag_at_v, 2)
    load_up = load(up, up_v, 3)
    load_inv = load(inv.at[0], inv_v, 4)
    load_down = load(down, down_v, 5)
    load_diag = load(diag.at[0], diag_v, 6)

    expected = 1 + has_next.astype(I32) + (far_end | second).astype(I32)
    line = len(same_z) * (z >= 1).astype(I32)
    for condition in (z == 0, z < DEPTH - 1, z >= 1, z >= 2, z >= 4):
        line += condition.astype(I32)
    expected += (1 - core) * line
    pl.semaphore_wait(barrier, expected)

    def remote(source, target, send, recv, device):
        return pltpu.make_async_remote_copy(
            src_ref=source,
            dst_ref=target,
            send_sem=send_sem.at[send],
            recv_sem=recv_sem.at[recv],
            device_id=device,
            device_id_type=MESH,
        )

    following = place_of(me + 1)
    halves = [pl.ds(0, FIRST_TILES), pl.ds(FIRST_TILES, KT - FIRST_TILES)]
    tall = [pl.ds(c * (P_SIZE // 2), P_SIZE // 2) for c in range(2)]
    send_inv = [
        remote(inv.at[0, rows], inv_in.at[rows], INV + c, INV + c, following)
        for c, rows in enumerate(tall)
    ]
    send_up = remote(up.at[1], up_in, UP, UP, following)
    send_places = remote(places, places_in, PLACE, PLACE, following)
    send_down = [
        remote(down.at[1, h], landing, DOWN + c, DOWN + c, following)
        for c, (h, landing) in enumerate(zip(halves, (first_in, down_in)))
    ]
    pieces = [pl.ds(p * (FIRST_TILES // 2), FIRST_TILES // 2) for p in range(2)]
    send_across = [
        remote(down.at[1, r], hop.at[r], HOP + p, HOP + p, other_core) for p, r in enumerate(pieces)
    ]
    send_over = [
        remote(hop.at[r], hop.at[r], HOP + p, HOP + p, middle) for p, r in enumerate(pieces)
    ]
    send_back = [
        remote(hop.at[r], hop.at[r], HOP + p, HOP + p, up_line(-3)) for p, r in enumerate(pieces)
    ]
    send_home = [
        remote(hop.at[r], first_in.at[r], HOP + p, HOME + p, up_line(-1))
        for p, r in enumerate(pieces)
    ]

    def forward(condition, copies):
        @pl.when(condition)
        def _():
            for arriving, copy in zip(send_across, copies):
                arriving.wait_recv()
                copy.start()

    @pl.when(giver)
    def _():
        for copy in send_across:
            copy.start()

    @pl.when(has_next)
    def _():
        send_inv[0].start()

    load_up_at.wait()
    load_down_at.wait()
    load_diag_at.wait()
    places[...] = jnp.full_like(places, -1)
    places[0:1] = slot_row(up_at_v[1:2])
    places[1:2] = slot_row(down_at_v[1:2])
    places[2:3] = slot_row(up_at_v[0:1])
    places[3:4] = slot_row(down_at_v[0:1])
    places[4:5] = slot_row(diag_at_v[...])
    places[5:6, 0:KT] = down_at_v[1:2]

    @pl.when(first_core & (z >= 1))
    def _():
        pl.semaphore_signal(near_sem, inc=1, device_id=up_line(-1), device_id_type=MESH)

    @pl.when(me == 0)
    def _():
        inv_in[...] = jnp.zeros_like(inv_in)
        up_in[...] = jnp.zeros_like(up_in)
        first_in[...] = jnp.zeros_like(first_in)
        down_in[...] = jnp.zeros_like(down_in)
        places_in[...] = jnp.zeros_like(places_in)

    load_slots = load(places, slots, 7)
    load_slots.wait()
    load_up.wait()
    expand(wide, lambda s: up_v[1, s], slots, 0)
    forward(far_end, send_over)
    load_inv.wait()

    def odd_product(cols):
        prod[:, cols] = mm(inv_v[...], wide[:, cols]).astype(BF16)

    column_blocks(odd_product)

    @pl.when(first_core & (z < DEPTH - 1))
    def _():
        pl.semaphore_wait(near_sem, 1)

    @pl.when(first_core & (z >= 2))
    def _():
        pl.semaphore_signal(far_sem, inc=1, device_id=up_line(-2), device_id_type=MESH)

    expand(even, lambda s: up_v[0, s], slots, 2)
    weight = (count + 2 * me).astype(F32) / count

    def up_product(cols):
        out = (-mm(even[...], prod[:, cols])).astype(BF16)
        new_up[:, cols] = out
        mean = jnp.sum(out.astype(F32), axis=0, keepdims=True) / P_SIZE
        term[:, cols] = weight * mean

    column_blocks(up_product)

    send_term = remote(term, pair_in, PAIR, PAIR, other_core)

    @pl.when(~first_core)
    def _():
        send_term.start()

    @pl.when(has_next)
    def _():
        send_inv[1].start()
        send_places.start()
        send_up.start()

    @pl.when(has_next & ~giver)
    def _():
        send_down[0].start()

    @pl.when(has_next)
    def _():
        send_down[1].start()

    load_down.wait()
    expand(wide, lambda s: down_v[1, s], slots, 1)
    send_pair = [
        remote(shared, columns_in.at[j], COLUMN + j, COLUMN + j, device)
        for j, device in enumerate(same_z)
    ]
    column_blocks(odd_product)

    @pl.when(first_core)
    def _():
        send_term.wait_recv()
        pair[...] = term[...] + pair_in[...]
        shared[...] = pair[...]

    send_first = remote(pair, first_total, FIRST, FIRST, up_line(1))

    @pl.when(first_core & (z == 0))
    def _():
        send_first.start()

    @pl.when(first_core & (z == 1))
    def _():
        send_first.wait_recv()
        shared[...] += first_total[...]

    @pl.when(meets)
    def _():
        for copy in send_pair:
            copy.start()

    @pl.when(first_core & (z < DEPTH - 2))
    def _():
        pl.semaphore_wait(far_sem, 1)

    load_diag.wait()
    expand(wide, lambda s: diag_v[s], slots, 4)

    def rest_product(cols):
        rest[:, cols] = wide[:, cols].astype(F32) - mm(even[...], prod[:, cols])

    column_blocks(rest_product)
    forward(second, send_back)

    before[...] = jnp.zeros_like(before)

    @pl.when(meets)
    def _():
        for copy in send_pair:
            copy.wait()
        for j in range(columns - 1):
            got = columns_in[j]
            before[...] += jnp.where(column > j, got, jnp.zeros_like(got))

    @pl.when(first_core & (z == 0))
    def _():
        send_first.wait_send()

    @pl.when(first_core)
    def _():
        rising[0] = before[...] + pair[...]
        falling[0] = before[...]

    def line_copies(n):
        up_step = remote(
            rising.at[n], rising_in.at[n], LINE + 2 * n, LINE + 2 * n, up_line(STEPS[n])
        )
        down_step = remote(
            falling.at[n],
            falling_in.at[n],
            LINE + 2 * n + 1,
            LINE + 2 * n + 1,
            up_line(-STEPS[n]),
        )
        return up_step, down_step

    def line_start(n):
        up_step, down_step = line_copies(n)

        @pl.when(first_core & (z + STEPS[n] < DEPTH))
        def _():
            up_step.start()

        @pl.when(first_core & (z >= STEPS[n]))
        def _():
            down_step.start()

    def line_finish(n):
        up_step, down_step = line_copies(n)
        last = n == len(STEPS) - 1
        if not last:
            rising[n + 1] = rising[n]
            falling[n + 1] = falling[n]

        @pl.when(first_core & (z >= STEPS[n]))
        def _():
            down_step.wait_send()
            up_step.wait_recv()
            before[...] += rising_in[n]
            if not last:
                rising[n + 1] += rising_in[n]

        @pl.when(first_core & (z + STEPS[n] < DEPTH))
        def _():
            up_step.wait_send()
            down_step.wait_recv()
            before[...] += falling_in[n]
            if not last:
                falling[n + 1] += falling_in[n]

    line_start(0)
    expand(even, lambda s: down_v[0, s], slots, 3)

    line_finish(0)
    line_start(1)

    @pl.when(has_prev)
    def _():
        for copy in send_inv:
            copy.wait_recv()

    def left_product(cols):
        left[:, cols] = mm(even[...], inv_in[:, cols]).astype(BF16)

    column_blocks(left_product, 2 * WIDE)
    forward(third, send_home)
    line_finish(1)
    line_start(2)
    line_finish(2)
    send_result = remote(upto, pair_in, RESULT, RESULT, other_core)

    @pl.when(first_core)
    def _():
        upto[...] = before[...] + term[...]
        sums[...] = upto[...]
        send_result.start()


    def lay_first(copies):
        for copy in copies:
            copy.wait_recv()
        expand(down_wide, lambda s: first_in[s], slots_in, 1, FIRST_TILES, unroll=True)

    @pl.when(has_prev)
    def _():
        send_places.wait_recv()

    load_slots_in = load(places_in, slots_in, 8)
    load_slots_in.wait()
    pl.when(hop_from)(functools.partial(lay_first, send_home))

    @pl.when(has_prev)
    def _():
        send_up.wait_recv()

    expand(wide, lambda s: up_in[s], slots_in, 0, unroll=True)

    def diag_product(cols):
        new_diag[:, cols] = (rest[:, cols] - mm(left[...], wide[:, cols])).astype(BF16)

    column_blocks(diag_product, 2 * WIDE)

    pl.when(has_prev & ~hop_from)(functools.partial(lay_first, send_down[:1]))

    @pl.when(me == 0)
    def _():
        down_wide[...] = jnp.zeros_like(down_wide)

    @pl.when(giver | far_end | second | third)
    def _():
        for copy in send_back:
            copy.wait_send()

    @pl.when(has_next & ~giver)
    def _():
        send_down[0].wait_send()

    @pl.when(has_next)
    def _():
        for copy in send_inv:
            copy.wait_send()
        send_up.wait_send()
        send_places.wait_send()
        send_down[1].wait_send()

    @pl.when(first_core)
    def _():
        send_result.wait_send()

    @pl.when(~first_core)
    def _():
        send_term.wait_send()
        send_result.wait_recv()
        sums[...] = term[...] + pair_in[...]

    @pl.when(has_prev)
    def _():
        send_down[1].wait_recv()


def exchange(sizes, *operands):
    dense = pltpu.VMEM((P_SIZE, P_SIZE), BF16)
    tiles = pltpu.VMEM((KT, TILE, TILE), BF16)
    half = pltpu.VMEM((FIRST_TILES, TILE, TILE), BF16)
    others = pltpu.VMEM((KT - FIRST_TILES, TILE, TILE), BF16)
    row = pltpu.VMEM((1, P_SIZE), F32)
    rows = pltpu.VMEM((len(STEPS), 1, P_SIZE), F32)
    columns = sizes[0] * sizes[1] // (2 * DEPTH)
    return pl.pallas_call(
        functools.partial(exchange_kernel, sizes),
        name="exchange",
        out_shape=(
            dense,
            dense,
            others,
            pltpu.SMEM((NT, TILE), I32),
            dense,
            dense,
            row,
        ),
        in_specs=[pl.BlockSpec(memory_space=pltpu.HBM)] * 7,
        out_specs=(pl.BlockSpec(memory_space=pltpu.VMEM),) * 3
        + (pl.BlockSpec(memory_space=pltpu.SMEM),)
        + (pl.BlockSpec(memory_space=pltpu.VMEM),) * 3,
        scratch_shapes=[
            pltpu.VMEM((2, KT), I32),
            pltpu.VMEM((2, KT), I32),
            pltpu.VMEM((1, KT), I32),
            pltpu.VMEM((2, KT, TILE, TILE), BF16),
            pltpu.VMEM((2, KT, TILE, TILE), BF16),
            tiles,
            dense,
            pltpu.VMEM((NT, TILE), I32),
            pltpu.SMEM((NT, TILE), I32),
            pltpu.VMEM((NT, TILE), I32),
            dense,
            tiles,
            half,
            half,
            dense,
            dense,
            dense,
            pltpu.VMEM((P_SIZE, P_SIZE), F32),
            row,
            row,
            row,
            row,
            row,
            row,
            row,
            pltpu.VMEM((columns - 1, 1, P_SIZE), F32),
            rows,
            rows,
            rows,
            rows,
            pltpu.SemaphoreType.DMA((9,)),
            pltpu.SemaphoreType.DMA((COLUMN + columns - 1,)),
            pltpu.SemaphoreType.DMA((COLUMN + columns - 1,)),
            pltpu.SemaphoreType.REGULAR,
            pltpu.SemaphoreType.REGULAR,
        ],
        compiler_params=pltpu.CompilerParams(
            collective_id=0, has_side_effects=True, vmem_limit_bytes=44 << 20
        ),
    )(*(pltpu.with_memory_space_constraint(x, pltpu.HBM) for x in operands))


def finish_kernel(
    places,
    left,
    wide_in,
    tiles,
    up_in,
    diag_in,
    sums_in,
    new_diag,
    new_up,
    new_down,
    sums,
    wide,
    out,
    sem,
):
    copies = [
        pltpu.make_async_copy(up_in, new_up.at[0], sem.at[0]),
        pltpu.make_async_copy(diag_in, new_diag.at[0], sem.at[1]),
    ]
    copies.append(pltpu.make_async_copy(sums_in, sums, sem.at[6]))
    for copy in copies:
        copy.start()
    for k in range(FIRST_TILES, KT):
        p = jnp.clip(places[5, k], 0, NT * NT - 1)
        r = pl.multiple_of((p >> 3) * TILE, TILE)
        c = pl.multiple_of((p & 7) * TILE, TILE)
        wide[pl.ds(r, TILE), pl.ds(c, TILE)] = tiles[k - FIRST_TILES]
    for b in range(P_SIZE // WIDE):
        rows = pl.ds(b * WIDE, WIDE)
        out[rows] = (-mm(left[rows], wide[...])).astype(BF16)
        copy = pltpu.make_async_copy(out.at[rows], new_down.at[0, rows], sem.at[2 + b])
        copy.start()
        copies.append(copy)
    for copy in copies:
        copy.wait()


def finish(places, left, wide, *operands):
    vmem = pl.BlockSpec(memory_space=pltpu.VMEM)
    hbm = pl.BlockSpec(memory_space=pltpu.HBM)
    square = jax.ShapeDtypeStruct((1, P_SIZE, P_SIZE), BF16)
    return pl.pallas_call(
        finish_kernel,
        name="finish",
        out_shape=(
            square,
            square,
            square,
            jax.ShapeDtypeStruct((1, P_SIZE), F32),
            pltpu.VMEM((P_SIZE, P_SIZE), BF16),
        ),
        in_specs=[pl.BlockSpec(memory_space=pltpu.SMEM)] + [vmem] * 6,
        out_specs=(hbm, hbm, hbm, hbm, vmem),
        scratch_shapes=[
            pltpu.VMEM((P_SIZE, P_SIZE), BF16),
            pltpu.SemaphoreType.DMA((3 + P_SIZE // WIDE,)),
        ],
        input_output_aliases={2: 4},
        compiler_params=pltpu.CompilerParams(vmem_limit_bytes=16 << 20),
    )(places, left, wide, *operands)


def local(sizes, up_tiles, up_at, down_tiles, down_at, diag_tiles, diag_at, odd_inverse):
    left, wide, down_in, places_in, new_up, new_diag, sums = exchange(
        sizes, up_at, down_at, diag_at, up_tiles, down_tiles, diag_tiles, odd_inverse
    )
    return finish(places_in, left, wide, down_in, new_up, new_diag, sums)[:4]


def solution(mesh):
    sizes = (mesh.shape["grp"], mesh.shape["lev"])
    return jax.shard_map(
        functools.partial(local, sizes),
        mesh=mesh,
        in_specs=(
            P(AXES, None, None, None),
            P(AXES, None),
            P(AXES, None, None, None),
            P(AXES, None),
            P(AXES, None, None, None),
            P(AXES, None),
            P(AXES, None, None),
        ),
        out_specs=(
            P(AXES, None, None),
            P(AXES, None, None),
            P(AXES, None, None),
            P(AXES, None),
        ),
        check_vma=False,
    )
```

```python
import functools

import jax
import jax.numpy as jnp
from jax import lax
from jax.experimental import pallas as pl
from jax.experimental.pallas import tpu as pltpu
from jax.sharding import PartitionSpec as P

TILE = 128
NT = 8
P_SIZE = 1024
KT = 24
FIRST_TILES = 16
WIDE = 256
HEIGHTS = (256, 256, 256, 128, 128)
DEPTH = 8
SIDE = 4
STEPS = (1, 2, 4)
AXES = ("grp", "lev")
MESH = pl.DeviceIdType.MESH
F32 = jnp.float32
BF16 = jnp.bfloat16
I32 = jnp.int32
INV, UP, PLACE, DOWN, HOP, HOME, PAIR, RESULT, FIRST, LINE, COLUMN = 0, 2, 3, 4, 6, 8, 10, 11, 12, 13, 19


def mm(a, b):
    return jnp.dot(a, b, preferred_element_type=F32)


def column_blocks(body, wide=WIDE):
    def step(b, carry):
        body(pl.ds(pl.multiple_of(b * wide, wide), wide))
        return carry

    lax.fori_loop(0, P_SIZE // wide, step, 0)


def expand(dense, tile_of, slots, row, below=KT, unroll=1):
    def tile_row(r, carry):
        rows = pl.ds(pl.multiple_of(r * TILE, TILE), TILE)
        for c in range(NT):
            slot = slots[row, r * NT + c]
            tile = tile_of(jnp.clip(slot, 0, below - 1))
            here = (slot >= 0) & (slot < below)
            dense[rows, c * TILE : (c + 1) * TILE] = jnp.where(here, tile, jnp.zeros_like(tile))
        return carry

    lax.fori_loop(0, NT, tile_row, 0, unroll=unroll)


def slot_row(places):
    number = lax.broadcasted_iota(I32, (KT, KT), 0)
    lane = lax.broadcasted_iota(I32, (KT, KT), 1)
    spread = jnp.broadcast_to(places, (KT, KT))
    column = jnp.sum(jnp.where(number == lane, spread, 0), axis=1, keepdims=True)
    position = lax.broadcasted_iota(I32, (KT, TILE), 1)
    index = lax.broadcasted_iota(I32, (KT, TILE), 0) + 1
    hit = jnp.broadcast_to(column, (KT, TILE)) == position
    return jnp.max(jnp.where(hit, index, 0), axis=0, keepdims=True) - 1


def exchange_kernel(
    sizes,
    up_at,
    down_at,
    diag_at,
    up,
    down,
    diag,
    inv,
    left,
    down_wide,
    down_in,
    slots_in,
    new_up,
    new_diag,
    sums,
    up_at_v,
    down_at_v,
    diag_at_v,
    up_v,
    down_v,
    diag_v,
    inv_v,
    places,
    slots,
    places_in,
    inv_in,
    up_in,
    first_in,
    hop,
    wide,
    even,
    prod,
    rest,
    term,
    pair,
    pair_in,
    before,
    upto,
    shared,
    first_total,
    columns_in,
    rising,
    falling,
    rising_in,
    falling_in,
    local_sem,
    send_sem,
    recv_sem,
    near_sem,
    far_sem,
):
    groups, inner = sizes
    count = groups * inner
    lev = lax.axis_index("lev")
    grp = lax.axis_index("grp")
    me = grp * inner + lev
    core = lev % 2
    z = (lev // 2) % DEPTH
    column = me // (2 * DEPTH)
    columns = count // (2 * DEPTH)

    def place_of(index):
        return (index // inner, index % inner)

    def up_line(distance):
        return place_of(me + 2 * distance)

    other_core = place_of(me + 1 - 2 * core)
    same_z = [
        place_of(((column + j) % columns) * 2 * DEPTH + 2 * z + core) for j in range(1, columns)
    ]
    has_next, has_prev = me < count - 1, me > 0
    inside = column < columns - 1
    first_core = core == 0
    meets = first_core & (z >= 1)
    giver = (core == 1) & (z == 7) & inside
    far_end = first_core & (z == 7) & inside
    second = first_core & (z == 4) & (column >= 1)
    third = first_core & (z == 1) & (column >= 1)
    hop_from = first_core & (z == 0) & has_prev
    middle = place_of((column + 1) * 2 * DEPTH + 8)
    giving = place_of((column - 1) * 2 * DEPTH + 14)

    def load(source, target, sem):
        copy = pltpu.make_async_copy(source, target, local_sem.at[sem])
        copy.start()
        return copy

    barrier = pltpu.get_barrier_semaphore()

    def tell(device):
        pl.semaphore_signal(barrier, inc=1, device_id=device, device_id_type=MESH)

    def tell_if(condition, device):
        @pl.when(condition)
        def _():
            tell(device)

    tell_if(has_prev, place_of(me - 1))
    tell(other_core)
    tell_if(first_core & (z >= 1), up_line(-1))
    for step in STEPS:
        tell_if(first_core & (z + step < DEPTH), up_line(step))
    tell_if(third, up_line(3))
    tell_if(second, giving)

    tell_if(first_core & (z == 1), up_line(-1))

    @pl.when(meets)
    def _():
        for device in same_z:
            tell(device)

    load_up_at = load(up_at, up_at_v, 0)
    load_down_at = load(down_at, down_at_v, 1)
    load_diag_at = load(diag_at, diag_at_v, 2)
    load_up = load(up, up_v, 3)
    load_inv = load(inv.at[0], inv_v, 4)
    load_down = load(down, down_v, 5)
    load_diag = load(diag.at[0], diag_v, 6)

    expected = 1 + has_next.astype(I32) + (far_end | second).astype(I32)
    line = len(same_z) * (z >= 1).astype(I32)
    for condition in (z == 0, z < DEPTH - 1, z >= 1, z >= 2, z >= 4):
        line += condition.astype(I32)
    expected += (1 - core) * line
    pl.semaphore_wait(barrier, expected)

    def remote(source, target, send, recv, device):
        return pltpu.make_async_remote_copy(
            src_ref=source,
            dst_ref=target,
            send_sem=send_sem.at[send],
            recv_sem=recv_sem.at[recv],
            device_id=device,
            device_id_type=MESH,
        )

    following = place_of(me + 1)
    halves = [pl.ds(0, FIRST_TILES), pl.ds(FIRST_TILES, KT - FIRST_TILES)]
    tall = [pl.ds(c * (P_SIZE // 2), P_SIZE // 2) for c in range(2)]
    send_inv = [
        remote(inv.at[0, rows], inv_in.at[rows], INV + c, INV + c, following)
        for c, rows in enumerate(tall)
    ]
    send_up = remote(up.at[1], up_in, UP, UP, following)
    send_places = remote(places, places_in, PLACE, PLACE, following)
    send_down = [
        remote(down.at[1, h], landing, DOWN + c, DOWN + c, following)
        for c, (h, landing) in enumerate(zip(halves, (first_in, down_in)))
    ]
    pieces = [pl.ds(p * (FIRST_TILES // 2), FIRST_TILES // 2) for p in range(2)]
    send_across = [
        remote(down.at[1, r], hop.at[r], HOP + p, HOP + p, other_core) for p, r in enumerate(pieces)
    ]
    send_over = [
        remote(hop.at[r], hop.at[r], HOP + p, HOP + p, middle) for p, r in enumerate(pieces)
    ]
    send_back = [
        remote(hop.at[r], hop.at[r], HOP + p, HOP + p, up_line(-3)) for p, r in enumerate(pieces)
    ]
    send_home = [
        remote(hop.at[r], first_in.at[r], HOP + p, HOME + p, up_line(-1))
        for p, r in enumerate(pieces)
    ]

    def forward(condition, copies, which=(0, 1)):
        @pl.when(condition)
        def _():
            for p in which:
                send_across[p].wait_recv()
                copies[p].start()

    @pl.when(giver)
    def _():
        for copy in send_across:
            copy.start()

    @pl.when(has_next)
    def _():
        send_inv[0].start()

    load_up_at.wait()
    load_down_at.wait()
    load_diag_at.wait()
    places[...] = jnp.full_like(places, -1)
    places[0:1] = slot_row(up_at_v[1:2])
    places[1:2] = slot_row(down_at_v[1:2])
    places[2:3] = slot_row(up_at_v[0:1])
    places[3:4] = slot_row(down_at_v[0:1])
    places[4:5] = slot_row(diag_at_v[...])
    places[5:6, 0:KT] = down_at_v[1:2]

    @pl.when(first_core & (z >= 1))
    def _():
        pl.semaphore_signal(near_sem, inc=1, device_id=up_line(-1), device_id_type=MESH)

    @pl.when(me == 0)
    def _():
        inv_in[...] = jnp.zeros_like(inv_in)
        up_in[...] = jnp.zeros_like(up_in)
        first_in[...] = jnp.zeros_like(first_in)
        down_in[...] = jnp.zeros_like(down_in)
        places_in[...] = jnp.zeros_like(places_in)

    load_slots = load(places, slots, 7)
    forward(far_end, send_over)
    load_slots.wait()
    load_up.wait()
    expand(wide, lambda s: up_v[1, s], slots, 0)
    load_inv.wait()

    def odd_product(cols):
        prod[:, cols] = mm(inv_v[...], wide[:, cols]).astype(BF16)

    column_blocks(odd_product)

    @pl.when(first_core & (z < DEPTH - 1))
    def _():
        pl.semaphore_wait(near_sem, 1)

    @pl.when(first_core & (z >= 2))
    def _():
        pl.semaphore_signal(far_sem, inc=1, device_id=up_line(-2), device_id_type=MESH)

    expand(even, lambda s: up_v[0, s], slots, 2)
    weight = (count + 2 * me).astype(F32) / count

    def up_product(cols):
        out = (-mm(even[...], prod[:, cols])).astype(BF16)
        new_up[:, cols] = out
        mean = jnp.sum(out.astype(F32), axis=0, keepdims=True) / P_SIZE
        term[:, cols] = weight * mean

    column_blocks(up_product)

    send_term = remote(term, pair_in, PAIR, PAIR, other_core)

    @pl.when(~first_core)
    def _():
        send_term.start()

    @pl.when(has_next)
    def _():
        send_inv[1].start()
        send_places.start()
        send_up.start()

    @pl.when(has_next & ~giver)
    def _():
        send_down[0].start()

    @pl.when(has_next)
    def _():
        send_down[1].start()

    load_down.wait()
    expand(wide, lambda s: down_v[1, s], slots, 1)
    send_pair = [
        remote(shared, columns_in.at[j], COLUMN + j, COLUMN + j, device)
        for j, device in enumerate(same_z)
    ]
    column_blocks(odd_product)

    @pl.when(first_core)
    def _():
        send_term.wait_recv()
        pair[...] = term[...] + pair_in[...]
        shared[...] = pair[...]

    send_first = remote(pair, first_total, FIRST, FIRST, up_line(1))

    @pl.when(first_core & (z == 0))
    def _():
        send_first.start()

    @pl.when(first_core & (z == 1))
    def _():
        send_first.wait_recv()
        shared[...] += first_total[...]

    @pl.when(meets)
    def _():
        for copy in send_pair:
            copy.start()

    @pl.when(first_core & (z < DEPTH - 2))
    def _():
        pl.semaphore_wait(far_sem, 1)

    load_diag.wait()
    expand(wide, lambda s: diag_v[s], slots, 4)

    def rest_product(cols):
        rest[:, cols] = wide[:, cols].astype(F32) - mm(even[...], prod[:, cols])

    forward(second, send_back, (0,))
    column_blocks(rest_product)
    forward(second, send_back, (1,))

    before[...] = jnp.zeros_like(before)

    @pl.when(meets)
    def _():
        for copy in send_pair:
            copy.wait()
        for j in range(columns - 1):
            got = columns_in[j]
            before[...] += jnp.where(column > j, got, jnp.zeros_like(got))

    @pl.when(first_core & (z == 0))
    def _():
        send_first.wait_send()

    @pl.when(first_core)
    def _():
        rising[0] = before[...] + pair[...]
        falling[0] = before[...]

    def line_copies(n):
        up_step = remote(
            rising.at[n], rising_in.at[n], LINE + 2 * n, LINE + 2 * n, up_line(STEPS[n])
        )
        down_step = remote(
            falling.at[n],
            falling_in.at[n],
            LINE + 2 * n + 1,
            LINE + 2 * n + 1,
            up_line(-STEPS[n]),
        )
        return up_step, down_step

    def line_start(n):
        up_step, down_step = line_copies(n)

        @pl.when(first_core & (z + STEPS[n] < DEPTH))
        def _():
            up_step.start()

        @pl.when(first_core & (z >= STEPS[n]))
        def _():
            down_step.start()

    def line_finish(n):
        up_step, down_step = line_copies(n)
        last = n == len(STEPS) - 1
        if not last:
            rising[n + 1] = rising[n]
            falling[n + 1] = falling[n]

        @pl.when(first_core & (z >= STEPS[n]))
        def _():
            down_step.wait_send()
            up_step.wait_recv()
            before[...] += rising_in[n]
            if not last:
                rising[n + 1] += rising_in[n]

        @pl.when(first_core & (z + STEPS[n] < DEPTH))
        def _():
            up_step.wait_send()
            down_step.wait_recv()
            before[...] += falling_in[n]
            if not last:
                falling[n + 1] += falling_in[n]

    line_start(0)
    expand(even, lambda s: down_v[0, s], slots, 3)

    line_finish(0)
    line_start(1)
    forward(third, send_home, (0,))

    @pl.when(has_prev)
    def _():
        for copy in send_inv:
            copy.wait_recv()

    def left_product(cols):
        left[:, cols] = mm(even[...], inv_in[:, cols]).astype(BF16)

    column_blocks(left_product, 2 * WIDE)
    forward(third, send_home, (1,))
    line_finish(1)
    line_start(2)
    line_finish(2)
    send_result = remote(upto, pair_in, RESULT, RESULT, other_core)

    @pl.when(first_core)
    def _():
        upto[...] = before[...] + term[...]
        sums[...] = upto[...]
        send_result.start()


    def lay_first(copies):
        for copy in copies:
            copy.wait_recv()
        expand(down_wide, lambda s: first_in[s], slots_in, 1, FIRST_TILES, unroll=True)

    @pl.when(has_prev)
    def _():
        send_places.wait_recv()

    load_slots_in = load(places_in, slots_in, 8)
    load_slots_in.wait()
    pl.when(hop_from)(functools.partial(lay_first, send_home))

    @pl.when(has_prev)
    def _():
        send_up.wait_recv()

    expand(wide, lambda s: up_in[s], slots_in, 0, unroll=True)

    def diag_product(cols):
        new_diag[:, cols] = (rest[:, cols] - mm(left[...], wide[:, cols])).astype(BF16)

    column_blocks(diag_product, 2 * WIDE)

    pl.when(has_prev & ~hop_from)(functools.partial(lay_first, send_down[:1]))

    @pl.when(me == 0)
    def _():
        down_wide[...] = jnp.zeros_like(down_wide)

    @pl.when(giver | far_end | second | third)
    def _():
        for copy in send_back:
            copy.wait_send()

    @pl.when(has_next & ~giver)
    def _():
        send_down[0].wait_send()

    @pl.when(has_next)
    def _():
        for copy in send_inv:
            copy.wait_send()
        send_up.wait_send()
        send_places.wait_send()
        send_down[1].wait_send()

    @pl.when(first_core)
    def _():
        send_result.wait_send()

    @pl.when(~first_core)
    def _():
        send_term.wait_send()
        send_result.wait_recv()
        sums[...] = term[...] + pair_in[...]

    @pl.when(has_prev)
    def _():
        send_down[1].wait_recv()


def exchange(sizes, *operands):
    dense = pltpu.VMEM((P_SIZE, P_SIZE), BF16)
    tiles = pltpu.VMEM((KT, TILE, TILE), BF16)
    half = pltpu.VMEM((FIRST_TILES, TILE, TILE), BF16)
    others = pltpu.VMEM((KT - FIRST_TILES, TILE, TILE), BF16)
    row = pltpu.VMEM((1, P_SIZE), F32)
    rows = pltpu.VMEM((len(STEPS), 1, P_SIZE), F32)
    columns = sizes[0] * sizes[1] // (2 * DEPTH)
    return pl.pallas_call(
        functools.partial(exchange_kernel, sizes),
        name="exchange",
        out_shape=(
            dense,
            dense,
            others,
            pltpu.SMEM((NT, TILE), I32),
            dense,
            dense,
            row,
        ),
        in_specs=[pl.BlockSpec(memory_space=pltpu.HBM)] * 7,
        out_specs=(pl.BlockSpec(memory_space=pltpu.VMEM),) * 3
        + (pl.BlockSpec(memory_space=pltpu.SMEM),)
        + (pl.BlockSpec(memory_space=pltpu.VMEM),) * 3,
        scratch_shapes=[
            pltpu.VMEM((2, KT), I32),
            pltpu.VMEM((2, KT), I32),
            pltpu.VMEM((1, KT), I32),
            pltpu.VMEM((2, KT, TILE, TILE), BF16),
            pltpu.VMEM((2, KT, TILE, TILE), BF16),
            tiles,
            dense,
            pltpu.VMEM((NT, TILE), I32),
            pltpu.SMEM((NT, TILE), I32),
            pltpu.VMEM((NT, TILE), I32),
            dense,
            tiles,
            half,
            half,
            dense,
            dense,
            dense,
            pltpu.VMEM((P_SIZE, P_SIZE), F32),
            row,
            row,
            row,
            row,
            row,
            row,
            row,
            pltpu.VMEM((columns - 1, 1, P_SIZE), F32),
            rows,
            rows,
            rows,
            rows,
            pltpu.SemaphoreType.DMA((9,)),
            pltpu.SemaphoreType.DMA((COLUMN + columns - 1,)),
            pltpu.SemaphoreType.DMA((COLUMN + columns - 1,)),
            pltpu.SemaphoreType.REGULAR,
            pltpu.SemaphoreType.REGULAR,
        ],
        compiler_params=pltpu.CompilerParams(
            collective_id=0, has_side_effects=True, vmem_limit_bytes=44 << 20
        ),
    )(*(pltpu.with_memory_space_constraint(x, pltpu.HBM) for x in operands))


def finish_kernel(
    places,
    left,
    wide_in,
    tiles,
    up_in,
    diag_in,
    sums_in,
    new_diag,
    new_up,
    new_down,
    sums,
    wide,
    out,
    sem,
):
    copies = [
        pltpu.make_async_copy(up_in, new_up.at[0], sem.at[0]),
        pltpu.make_async_copy(diag_in, new_diag.at[0], sem.at[1]),
    ]
    copies.append(pltpu.make_async_copy(sums_in, sums, sem.at[2]))
    for copy in copies:
        copy.start()
    for k in range(FIRST_TILES, KT):
        p = jnp.clip(places[5, k], 0, NT * NT - 1)
        r = pl.multiple_of((p >> 3) * TILE, TILE)
        c = pl.multiple_of((p & 7) * TILE, TILE)
        wide[pl.ds(r, TILE), pl.ds(c, TILE)] = tiles[k - FIRST_TILES]
    start = 0
    for b, height in enumerate(HEIGHTS):
        rows = pl.ds(start, height)
        out[rows] = (-mm(left[rows], wide[...])).astype(BF16)
        copy = pltpu.make_async_copy(out.at[rows], new_down.at[0, rows], sem.at[3 + b])
        copy.start()
        copies.append(copy)
        start += height
    for copy in copies:
        copy.wait()


def finish(places, left, wide, *operands):
    vmem = pl.BlockSpec(memory_space=pltpu.VMEM)
    hbm = pl.BlockSpec(memory_space=pltpu.HBM)
    square = jax.ShapeDtypeStruct((1, P_SIZE, P_SIZE), BF16)
    return pl.pallas_call(
        finish_kernel,
        name="finish",
        out_shape=(
            square,
            square,
            square,
            jax.ShapeDtypeStruct((1, P_SIZE), F32),
            pltpu.VMEM((P_SIZE, P_SIZE), BF16),
        ),
        in_specs=[pl.BlockSpec(memory_space=pltpu.SMEM)] + [vmem] * 6,
        out_specs=(hbm, hbm, hbm, hbm, vmem),
        scratch_shapes=[
            pltpu.VMEM((P_SIZE, P_SIZE), BF16),
            pltpu.SemaphoreType.DMA((3 + len(HEIGHTS),)),
        ],
        input_output_aliases={2: 4},
        compiler_params=pltpu.CompilerParams(vmem_limit_bytes=16 << 20),
    )(places, left, wide, *operands)


def local(sizes, up_tiles, up_at, down_tiles, down_at, diag_tiles, diag_at, odd_inverse):
    left, wide, down_in, places_in, new_up, new_diag, sums = exchange(
        sizes, up_at, down_at, diag_at, up_tiles, down_tiles, diag_tiles, odd_inverse
    )
    return finish(places_in, left, wide, down_in, new_up, new_diag, sums)[:4]


def solution(mesh):
    sizes = (mesh.shape["grp"], mesh.shape["lev"])
    return jax.shard_map(
        functools.partial(local, sizes),
        mesh=mesh,
        in_specs=(
            P(AXES, None, None, None),
            P(AXES, None),
            P(AXES, None, None, None),
            P(AXES, None),
            P(AXES, None, None, None),
            P(AXES, None),
            P(AXES, None, None),
        ),
        out_specs=(
            P(AXES, None, None),
            P(AXES, None, None),
            P(AXES, None, None),
            P(AXES, None),
        ),
        check_vma=False,
    )
```

```python
import functools

import jax
import jax.numpy as jnp
from jax import lax
from jax.experimental import pallas as pl
from jax.experimental.pallas import tpu as pltpu
from jax.sharding import PartitionSpec as P

TILE = 128
NT = 8
P_SIZE = 1024
KT = 24
FIRST_TILES = 16
WIDE = 256
HEIGHTS = (256, 256, 256, 128, 128)
DEPTH = 8
SIDE = 4
STEPS = (1, 2, 4)
AXES = ("grp", "lev")
MESH = pl.DeviceIdType.MESH
F32 = jnp.float32
BF16 = jnp.bfloat16
I32 = jnp.int32
INV, UP, PLACE, DOWN, HOP, HOME, PAIR, RESULT, FIRST, LINE, COLUMN = 0, 2, 3, 4, 6, 8, 10, 11, 12, 13, 19


def mm(a, b):
    return jnp.dot(a, b, preferred_element_type=F32)


def column_blocks(body, wide=WIDE):
    def step(b, carry):
        body(pl.ds(pl.multiple_of(b * wide, wide), wide))
        return carry

    lax.fori_loop(0, P_SIZE // wide, step, 0)


def expand(dense, tile_of, slots, row, below=KT, unroll=1):
    def tile_row(r, carry):
        rows = pl.ds(pl.multiple_of(r * TILE, TILE), TILE)
        for c in range(NT):
            slot = slots[row, r * NT + c]
            tile = tile_of(jnp.clip(slot, 0, below - 1))
            here = (slot >= 0) & (slot < below)
            dense[rows, c * TILE : (c + 1) * TILE] = jnp.where(here, tile, jnp.zeros_like(tile))
        return carry

    lax.fori_loop(0, NT, tile_row, 0, unroll=unroll)


def slot_row(places):
    number = lax.broadcasted_iota(I32, (KT, KT), 0)
    lane = lax.broadcasted_iota(I32, (KT, KT), 1)
    spread = jnp.broadcast_to(places, (KT, KT))
    column = jnp.sum(jnp.where(number == lane, spread, 0), axis=1, keepdims=True)
    position = lax.broadcasted_iota(I32, (KT, TILE), 1)
    index = lax.broadcasted_iota(I32, (KT, TILE), 0) + 1
    hit = jnp.broadcast_to(column, (KT, TILE)) == position
    return jnp.max(jnp.where(hit, index, 0), axis=0, keepdims=True) - 1


def exchange_kernel(
    sizes,
    up_at,
    down_at,
    diag_at,
    up,
    down,
    diag,
    inv,
    left,
    down_wide,
    down_in,
    slots_in,
    new_up,
    new_diag,
    sums,
    up_at_v,
    down_at_v,
    diag_at_v,
    up_v,
    down_v,
    diag_v,
    inv_v,
    places,
    slots,
    places_in,
    inv_in,
    up_in,
    first_in,
    hop,
    wide,
    even,
    prod,
    rest,
    term,
    pair,
    pair_in,
    before,
    upto,
    shared,
    first_total,
    columns_in,
    rising,
    falling,
    rising_in,
    falling_in,
    local_sem,
    send_sem,
    recv_sem,
    near_sem,
    far_sem,
):
    groups, inner = sizes
    count = groups * inner
    lev = lax.axis_index("lev")
    grp = lax.axis_index("grp")
    me = grp * inner + lev
    core = lev % 2
    z = (lev // 2) % DEPTH
    column = me // (2 * DEPTH)
    columns = count // (2 * DEPTH)

    def place_of(index):
        return (index // inner, index % inner)

    def up_line(distance):
        return place_of(me + 2 * distance)

    other_core = place_of(me + 1 - 2 * core)
    same_z = [
        place_of(((column + j) % columns) * 2 * DEPTH + 2 * z + core) for j in range(1, columns)
    ]
    has_next, has_prev = me < count - 1, me > 0
    inside = column < columns - 1
    first_core = core == 0
    meets = first_core & (z >= 1)
    giver = (core == 1) & (z == 7) & inside
    far_end = first_core & (z == 7) & inside
    second = first_core & (z == 4) & (column >= 1)
    third = first_core & (z == 1) & (column >= 1)
    hop_from = first_core & (z == 0) & has_prev
    middle = place_of((column + 1) * 2 * DEPTH + 8)
    giving = place_of((column - 1) * 2 * DEPTH + 14)

    def load(source, target, sem):
        copy = pltpu.make_async_copy(source, target, local_sem.at[sem])
        copy.start()
        return copy

    barrier = pltpu.get_barrier_semaphore()

    def tell(device):
        pl.semaphore_signal(barrier, inc=1, device_id=device, device_id_type=MESH)

    def tell_if(condition, device):
        @pl.when(condition)
        def _():
            tell(device)

    tell_if(has_prev, place_of(me - 1))
    tell(other_core)
    tell_if(first_core & (z >= 1), up_line(-1))
    for step in STEPS:
        tell_if(first_core & (z + step < DEPTH), up_line(step))
    tell_if(third, up_line(3))
    tell_if(second, giving)

    tell_if(first_core & (z == 1), up_line(-1))

    @pl.when(meets)
    def _():
        for device in same_z:
            tell(device)

    load_up_at = load(up_at, up_at_v, 0)
    load_down_at = load(down_at, down_at_v, 1)
    load_diag_at = load(diag_at, diag_at_v, 2)
    load_up = load(up, up_v, 3)
    load_inv = load(inv.at[0], inv_v, 4)

    expected = 1 + has_next.astype(I32) + (far_end | second).astype(I32)
    line = len(same_z) * (z >= 1).astype(I32)
    for condition in (z == 0, z < DEPTH - 1, z >= 1, z >= 2, z >= 4):
        line += condition.astype(I32)
    expected += (1 - core) * line
    pl.semaphore_wait(barrier, expected)

    def remote(source, target, send, recv, device):
        return pltpu.make_async_remote_copy(
            src_ref=source,
            dst_ref=target,
            send_sem=send_sem.at[send],
            recv_sem=recv_sem.at[recv],
            device_id=device,
            device_id_type=MESH,
        )

    following = place_of(me + 1)
    halves = [pl.ds(0, FIRST_TILES), pl.ds(FIRST_TILES, KT - FIRST_TILES)]
    tall = [pl.ds(c * (P_SIZE // 2), P_SIZE // 2) for c in range(2)]
    send_inv = [
        remote(inv.at[0, rows], inv_in.at[rows], INV + c, INV + c, following)
        for c, rows in enumerate(tall)
    ]
    send_up = remote(up.at[1], up_in, UP, UP, following)
    send_places = remote(places, places_in, PLACE, PLACE, following)
    send_down = [
        remote(down.at[1, h], landing, DOWN + c, DOWN + c, following)
        for c, (h, landing) in enumerate(zip(halves, (first_in, down_in)))
    ]
    pieces = [pl.ds(p * (FIRST_TILES // 2), FIRST_TILES // 2) for p in range(2)]
    send_across = [
        remote(down.at[1, r], hop.at[r], HOP + p, HOP + p, other_core) for p, r in enumerate(pieces)
    ]
    send_over = [
        remote(hop.at[r], hop.at[r], HOP + p, HOP + p, middle) for p, r in enumerate(pieces)
    ]
    send_back = [
        remote(hop.at[r], hop.at[r], HOP + p, HOP + p, up_line(-3)) for p, r in enumerate(pieces)
    ]
    send_home = [
        remote(hop.at[r], first_in.at[r], HOP + p, HOME + p, up_line(-1))
        for p, r in enumerate(pieces)
    ]

    def forward(condition, copies, which=(0, 1)):
        @pl.when(condition)
        def _():
            for p in which:
                send_across[p].wait_recv()
                copies[p].start()

    @pl.when(giver)
    def _():
        for copy in send_across:
            copy.start()

    @pl.when(has_next)
    def _():
        send_inv[0].start()

    load_down = load(down, down_v, 5)
    load_diag = load(diag.at[0], diag_v, 6)
    load_up_at.wait()
    load_down_at.wait()
    load_diag_at.wait()
    places[...] = jnp.full_like(places, -1)
    places[0:1] = slot_row(up_at_v[1:2])
    places[1:2] = slot_row(down_at_v[1:2])
    places[2:3] = slot_row(up_at_v[0:1])
    places[3:4] = slot_row(down_at_v[0:1])
    places[4:5] = slot_row(diag_at_v[...])
    places[5:6, 0:KT] = down_at_v[1:2]

    @pl.when(first_core & (z >= 1))
    def _():
        pl.semaphore_signal(near_sem, inc=1, device_id=up_line(-1), device_id_type=MESH)

    @pl.when(me == 0)
    def _():
        inv_in[...] = jnp.zeros_like(inv_in)
        up_in[...] = jnp.zeros_like(up_in)
        first_in[...] = jnp.zeros_like(first_in)
        down_in[...] = jnp.zeros_like(down_in)
        places_in[...] = jnp.zeros_like(places_in)

    load_slots = load(places, slots, 7)
    forward(far_end, send_over)
    load_slots.wait()
    load_up.wait()
    expand(wide, lambda s: up_v[1, s], slots, 0)
    load_inv.wait()

    def odd_product(cols):
        prod[:, cols] = mm(inv_v[...], wide[:, cols]).astype(BF16)

    column_blocks(odd_product)

    @pl.when(first_core & (z < DEPTH - 1))
    def _():
        pl.semaphore_wait(near_sem, 1)

    @pl.when(first_core & (z >= 2))
    def _():
        pl.semaphore_signal(far_sem, inc=1, device_id=up_line(-2), device_id_type=MESH)

    expand(even, lambda s: up_v[0, s], slots, 2)
    weight = (count + 2 * me).astype(F32) / count

    def up_product(cols):
        out = (-mm(even[...], prod[:, cols])).astype(BF16)
        new_up[:, cols] = out
        mean = jnp.sum(out.astype(F32), axis=0, keepdims=True) / P_SIZE
        term[:, cols] = weight * mean

    column_blocks(up_product)

    send_term = remote(term, pair_in, PAIR, PAIR, other_core)

    @pl.when(~first_core)
    def _():
        send_term.start()

    @pl.when(has_next)
    def _():
        send_inv[1].start()
        send_places.start()
        send_up.start()

    @pl.when(has_next & ~giver)
    def _():
        send_down[0].start()

    @pl.when(has_next)
    def _():
        send_down[1].start()

    load_down.wait()
    expand(wide, lambda s: down_v[1, s], slots, 1)
    send_pair = [
        remote(shared, columns_in.at[j], COLUMN + j, COLUMN + j, device)
        for j, device in enumerate(same_z)
    ]
    column_blocks(odd_product)

    @pl.when(first_core)
    def _():
        send_term.wait_recv()
        pair[...] = term[...] + pair_in[...]
        shared[...] = pair[...]

    send_first = remote(pair, first_total, FIRST, FIRST, up_line(1))

    @pl.when(first_core & (z == 0))
    def _():
        send_first.start()

    @pl.when(first_core & (z == 1))
    def _():
        send_first.wait_recv()
        shared[...] += first_total[...]

    @pl.when(meets)
    def _():
        for copy in send_pair:
            copy.start()

    @pl.when(first_core & (z < DEPTH - 2))
    def _():
        pl.semaphore_wait(far_sem, 1)

    load_diag.wait()
    expand(wide, lambda s: diag_v[s], slots, 4)

    def rest_product(cols):
        rest[:, cols] = wide[:, cols].astype(F32) - mm(even[...], prod[:, cols])

    forward(second, send_back, (0,))
    column_blocks(rest_product)
    forward(second, send_back, (1,))

    before[...] = jnp.zeros_like(before)

    @pl.when(meets)
    def _():
        for copy in send_pair:
            copy.wait()
        for j in range(columns - 1):
            got = columns_in[j]
            before[...] += jnp.where(column > j, got, jnp.zeros_like(got))

    @pl.when(first_core & (z == 0))
    def _():
        send_first.wait_send()

    @pl.when(first_core)
    def _():
        rising[0] = before[...] + pair[...]
        falling[0] = before[...]

    def line_copies(n):
        up_step = remote(
            rising.at[n], rising_in.at[n], LINE + 2 * n, LINE + 2 * n, up_line(STEPS[n])
        )
        down_step = remote(
            falling.at[n],
            falling_in.at[n],
            LINE + 2 * n + 1,
            LINE + 2 * n + 1,
            up_line(-STEPS[n]),
        )
        return up_step, down_step

    def line_start(n):
        up_step, down_step = line_copies(n)

        @pl.when(first_core & (z + STEPS[n] < DEPTH))
        def _():
            up_step.start()

        @pl.when(first_core & (z >= STEPS[n]))
        def _():
            down_step.start()

    def line_finish(n):
        up_step, down_step = line_copies(n)
        last = n == len(STEPS) - 1
        if not last:
            rising[n + 1] = rising[n]
            falling[n + 1] = falling[n]

        @pl.when(first_core & (z >= STEPS[n]))
        def _():
            down_step.wait_send()
            up_step.wait_recv()
            before[...] += rising_in[n]
            if not last:
                rising[n + 1] += rising_in[n]

        @pl.when(first_core & (z + STEPS[n] < DEPTH))
        def _():
            up_step.wait_send()
            down_step.wait_recv()
            before[...] += falling_in[n]
            if not last:
                falling[n + 1] += falling_in[n]

    line_start(0)
    expand(even, lambda s: down_v[0, s], slots, 3)

    line_finish(0)
    line_start(1)
    forward(third, send_home, (0,))

    @pl.when(has_prev)
    def _():
        for copy in send_inv:
            copy.wait_recv()

    def left_product(cols):
        left[:, cols] = mm(even[...], inv_in[:, cols]).astype(BF16)

    column_blocks(left_product, 2 * WIDE)
    forward(third, send_home, (1,))
    line_finish(1)
    line_start(2)
    line_finish(2)
    send_result = remote(upto, pair_in, RESULT, RESULT, other_core)

    @pl.when(first_core)
    def _():
        upto[...] = before[...] + term[...]
        sums[...] = upto[...]
        send_result.start()


    def lay_first(copies):
        for copy in copies:
            copy.wait_recv()
        expand(down_wide, lambda s: first_in[s], slots_in, 1, FIRST_TILES, unroll=True)

    @pl.when(has_prev)
    def _():
        send_places.wait_recv()

    load_slots_in = load(places_in, slots_in, 8)
    load_slots_in.wait()
    pl.when(hop_from)(functools.partial(lay_first, send_home))

    @pl.when(has_prev)
    def _():
        send_up.wait_recv()

    expand(wide, lambda s: up_in[s], slots_in, 0, unroll=True)

    def diag_product(cols):
        new_diag[:, cols] = (rest[:, cols] - mm(left[...], wide[:, cols])).astype(BF16)

    column_blocks(diag_product, 2 * WIDE)

    pl.when(has_prev & ~hop_from)(functools.partial(lay_first, send_down[:1]))

    @pl.when(me == 0)
    def _():
        down_wide[...] = jnp.zeros_like(down_wide)

    @pl.when(giver | far_end | second | third)
    def _():
        for copy in send_back:
            copy.wait_send()

    @pl.when(has_next & ~giver)
    def _():
        send_down[0].wait_send()

    @pl.when(has_next)
    def _():
        for copy in send_inv:
            copy.wait_send()
        send_up.wait_send()
        send_places.wait_send()
        send_down[1].wait_send()

    @pl.when(first_core)
    def _():
        send_result.wait_send()

    @pl.when(~first_core)
    def _():
        send_term.wait_send()
        send_result.wait_recv()
        sums[...] = term[...] + pair_in[...]

    @pl.when(has_prev)
    def _():
        send_down[1].wait_recv()


def exchange(sizes, *operands):
    dense = pltpu.VMEM((P_SIZE, P_SIZE), BF16)
    tiles = pltpu.VMEM((KT, TILE, TILE), BF16)
    half = pltpu.VMEM((FIRST_TILES, TILE, TILE), BF16)
    others = pltpu.VMEM((KT - FIRST_TILES, TILE, TILE), BF16)
    row = pltpu.VMEM((1, P_SIZE), F32)
    rows = pltpu.VMEM((len(STEPS), 1, P_SIZE), F32)
    columns = sizes[0] * sizes[1] // (2 * DEPTH)
    return pl.pallas_call(
        functools.partial(exchange_kernel, sizes),
        name="exchange",
        out_shape=(
            dense,
            dense,
            others,
            pltpu.SMEM((NT, TILE), I32),
            dense,
            dense,
            row,
        ),
        in_specs=[pl.BlockSpec(memory_space=pltpu.HBM)] * 7,
        out_specs=(pl.BlockSpec(memory_space=pltpu.VMEM),) * 3
        + (pl.BlockSpec(memory_space=pltpu.SMEM),)
        + (pl.BlockSpec(memory_space=pltpu.VMEM),) * 3,
        scratch_shapes=[
            pltpu.VMEM((2, KT), I32),
            pltpu.VMEM((2, KT), I32),
            pltpu.VMEM((1, KT), I32),
            pltpu.VMEM((2, KT, TILE, TILE), BF16),
            pltpu.VMEM((2, KT, TILE, TILE), BF16),
            tiles,
            dense,
            pltpu.VMEM((NT, TILE), I32),
            pltpu.SMEM((NT, TILE), I32),
            pltpu.VMEM((NT, TILE), I32),
            dense,
            tiles,
            half,
            half,
            dense,
            dense,
            dense,
            pltpu.VMEM((P_SIZE, P_SIZE), F32),
            row,
            row,
            row,
            row,
            row,
            row,
            row,
            pltpu.VMEM((columns - 1, 1, P_SIZE), F32),
            rows,
            rows,
            rows,
            rows,
            pltpu.SemaphoreType.DMA((9,)),
            pltpu.SemaphoreType.DMA((COLUMN + columns - 1,)),
            pltpu.SemaphoreType.DMA((COLUMN + columns - 1,)),
            pltpu.SemaphoreType.REGULAR,
            pltpu.SemaphoreType.REGULAR,
        ],
        compiler_params=pltpu.CompilerParams(
            collective_id=0, has_side_effects=True, vmem_limit_bytes=44 << 20
        ),
    )(*(pltpu.with_memory_space_constraint(x, pltpu.HBM) for x in operands))


def finish_kernel(
    places,
    left,
    wide_in,
    tiles,
    up_in,
    diag_in,
    sums_in,
    new_diag,
    new_up,
    new_down,
    sums,
    wide,
    out,
    sem,
):
    copies = [
        pltpu.make_async_copy(up_in, new_up.at[0], sem.at[0]),
        pltpu.make_async_copy(diag_in, new_diag.at[0], sem.at[1]),
    ]
    copies.append(pltpu.make_async_copy(sums_in, sums, sem.at[2]))
    for copy in copies:
        copy.start()
    for k in range(FIRST_TILES, KT):
        p = jnp.clip(places[5, k], 0, NT * NT - 1)
        r = pl.multiple_of((p >> 3) * TILE, TILE)
        c = pl.multiple_of((p & 7) * TILE, TILE)
        wide[pl.ds(r, TILE), pl.ds(c, TILE)] = tiles[k - FIRST_TILES]
    start = 0
    for b, height in enumerate(HEIGHTS):
        rows = pl.ds(start, height)
        out[rows] = (-mm(left[rows], wide[...])).astype(BF16)
        copy = pltpu.make_async_copy(out.at[rows], new_down.at[0, rows], sem.at[3 + b])
        copy.start()
        copies.append(copy)
        start += height
    for copy in copies:
        copy.wait()


def finish(places, left, wide, *operands):
    vmem = pl.BlockSpec(memory_space=pltpu.VMEM)
    hbm = pl.BlockSpec(memory_space=pltpu.HBM)
    square = jax.ShapeDtypeStruct((1, P_SIZE, P_SIZE), BF16)
    return pl.pallas_call(
        finish_kernel,
        name="finish",
        out_shape=(
            square,
            square,
            square,
            jax.ShapeDtypeStruct((1, P_SIZE), F32),
            pltpu.VMEM((P_SIZE, P_SIZE), BF16),
        ),
        in_specs=[pl.BlockSpec(memory_space=pltpu.SMEM)] + [vmem] * 6,
        out_specs=(hbm, hbm, hbm, hbm, vmem),
        scratch_shapes=[
            pltpu.VMEM((P_SIZE, P_SIZE), BF16),
            pltpu.SemaphoreType.DMA((3 + len(HEIGHTS),)),
        ],
        input_output_aliases={2: 4},
        compiler_params=pltpu.CompilerParams(vmem_limit_bytes=16 << 20),
    )(places, left, wide, *operands)


def local(sizes, up_tiles, up_at, down_tiles, down_at, diag_tiles, diag_at, odd_inverse):
    left, wide, down_in, places_in, new_up, new_diag, sums = exchange(
        sizes, up_at, down_at, diag_at, up_tiles, down_tiles, diag_tiles, odd_inverse
    )
    return finish(places_in, left, wide, down_in, new_up, new_diag, sums)[:4]


def solution(mesh):
    sizes = (mesh.shape["grp"], mesh.shape["lev"])
    return jax.shard_map(
        functools.partial(local, sizes),
        mesh=mesh,
        in_specs=(
            P(AXES, None, None, None),
            P(AXES, None),
            P(AXES, None, None, None),
            P(AXES, None),
            P(AXES, None, None, None),
            P(AXES, None),
            P(AXES, None, None),
        ),
        out_specs=(
            P(AXES, None, None),
            P(AXES, None, None),
            P(AXES, None, None),
            P(AXES, None),
        ),
        check_vma=False,
    )
```
